256 devices in a mesh: dp: 2 (over z_lo), chan: 8 (over z_hi, core), seq: 16 (over y, x).
Axes of the slice: x: 4, y: 4, z: 8 (z_hi: 4, z_lo: 2; z = z_hi * 2 + z_lo), core: 2. Of those that a mesh axis runs over, the one named last changes fastest.
Arguments:
- query_proj: bfloat16 [2, 2048, 8192], P('dp', 'chan', 'seq'), may hold values from -6 to 6
- key_proj: bfloat16 [2, 2048, 8192], P('dp', 'chan', 'seq'), may hold values from -6 to 6
- value_proj: bfloat16 [2, 2048, 8192], P('dp', 'chan', 'seq'), may hold values from -6 to 6
- grad_out: bfloat16 [2, 2048, 8192], P('dp', 'chan', 'seq'), may hold values from -6 to 6
- out_weight: bfloat16 [2048, 2048], P('chan'), may hold values from -0.125 to 0.125
- long_filter: float32 [2048, 8192], P(('chan', 'seq')), may hold values from -2 to 2, as said below
Outputs:
- grad_query: bfloat16 [2, 2048, 8192], P('dp', 'chan', 'seq')
- grad_key: bfloat16 [2, 2048, 8192], P('dp', 'chan', 'seq')
- grad_value: bfloat16 [2, 2048, 8192], P('dp', 'chan', 'seq')
- grad_weight: float32 [2048, 2048], P('chan')
The draws below stay inside these ranges and needn't reach their ends.
Inputs may be any that keep to these rules, and one draw needn't show every extreme that they name: `long_filter`: taps of each channel's causal filter.
All inputs are finite; a program needn't handle non-finite values.
Results may differ from the reference program's by a relative error of at most 0.0029.
Values may be sent and summed in bfloat16 or wider, within the bound.
No kernel may reach another device: no remote copies, remote signals or barrier semaphores. Data moves between devices by JAX's collectives and lax.ppermute only.
A program may use at most 64 MiB of HBM per device.

```python
import math
import jax
import jax.numpy as jnp
from jax import lax

CH = 2048
SEQLEN = 8192
BATCH = 2


def draw_long_filter(key, part):
    key_kind, key_slow, key_fast, key_noise = jax.random.split(key, 4)
    share = 0.5
    noise = jnp.clip(jax.random.normal(key_noise, (CH, SEQLEN), jnp.float32), -6.0, 6.0)
    slow_mask = jax.random.bernoulli(key_kind, share, (CH, 1))
    slow_rate = jnp.exp(jax.random.uniform(key_slow, (CH, 1), jnp.float32, math.log(0.3), math.log(2.0))) / SEQLEN
    fast_rate = jnp.exp(jax.random.uniform(key_fast, (CH, 1), jnp.float32, math.log(1.0 / 50.0), math.log(1.0 / 30.0)))
    rate = jnp.where(slow_mask, slow_rate, fast_rate)
    positions = lax.broadcasted_iota(jnp.float32, (CH, SEQLEN), 1)
    amplitude = jnp.sqrt(2.0 * rate / (1.0 - jnp.exp(-2.0 * rate * SEQLEN)))
    return (noise * amplitude * jnp.exp(-rate * positions)).astype(jnp.float32)


def shard_levels(own_key, shape, cuts, least, high):
    factor_of = 1.0
    for position, blocks in cuts:
        draws = jax.random.uniform(jax.random.fold_in(jax.random.fold_in(own_key, 6), position), (blocks,), jnp.float32, least / len(cuts), high / len(cuts))
        factor_of = factor_of * jnp.repeat(jnp.exp(draws), shape[position] // blocks).reshape((-1,) + (1,) * (len(shape) - 1 - position))
    return factor_of


def gaussian(own_key, shape, width, reach, shards=(), dtype=jnp.bfloat16):
    drawn = width * jax.random.normal(own_key, shape, jnp.float32)
    if shards:
        drawn = drawn * shard_levels(own_key, shape, shards, -0.22, 0.18)
    return jnp.clip(drawn, -reach, reach).astype(dtype)


def setup_inputs(seed: int = 0) -> dict:
    arg_keys = jax.random.split(jax.random.key(seed), 7)
    return {
        "query_proj": gaussian(arg_keys[0], (BATCH, CH, SEQLEN), 1.0, 6.0, ((0, 2), (1, 8), (2, 16))),
        "key_proj": gaussian(arg_keys[1], (BATCH, CH, SEQLEN), 1.0, 6.0, ((0, 2), (1, 8), (2, 16))),
        "value_proj": gaussian(arg_keys[2], (BATCH, CH, SEQLEN), 1.0, 6.0, ((0, 2), (1, 8), (2, 16))),
        "grad_out": gaussian(arg_keys[3], (BATCH, CH, SEQLEN), 1.0, 6.0, ((0, 2), (1, 8), (2, 16))),
        "out_weight": gaussian(arg_keys[4], (CH, CH), CH ** -0.5, 0.125, ((0, 8),)),
        "long_filter": draw_long_filter(jax.random.fold_in(arg_keys[6], 71), 0),
    }


def spectral(filt_rows, signal, conjugate):
    length = signal.shape[-1]
    total_len = 2 * length
    filt_spec = jnp.fft.rfft(filt_rows, n=total_len)
    signal_spec = jnp.fft.rfft(signal, n=total_len)
    if conjugate:
        filt_spec = jnp.conj(filt_spec)
    return jnp.fft.irfft(signal_spec * filt_spec, n=total_len)[..., :length]

def channel_map(long_filter, signal, conjugate):
    group_size = min(CH, 128)
    filt_blocks = long_filter.reshape(CH // group_size, group_size, SEQLEN)
    signal_blocks = signal.reshape(CH // group_size, group_size, SEQLEN)
    result = lax.map(lambda pair: spectral(pair[0], pair[1], conjugate), (filt_blocks, signal_blocks))
    return result.reshape(CH, SEQLEN).astype(jnp.float32)

def reference(query_proj, key_proj, value_proj, grad_out, out_weight, long_filter):
    weight_total = jnp.zeros((CH, CH), jnp.float32)
    query_list = []
    key_list = []
    value_list = []
    for seq_index in range(BATCH):
        query_vals = query_proj[seq_index].astype(jnp.float32)
        key_vals = key_proj[seq_index].astype(jnp.float32)
        value_vals = value_proj[seq_index].astype(jnp.float32)
        mixed_in = key_vals * value_vals
        conv_out = channel_map(long_filter, mixed_in, False)
        gated_out = (query_vals * conv_out).astype(jnp.bfloat16)
        grad_mid = jnp.dot(out_weight, grad_out[seq_index], preferred_element_type=jnp.float32)
        weight_total = weight_total + lax.dot_general(gated_out, grad_out[seq_index], (((1,), (1,)), ((), ())), preferred_element_type=jnp.float32)
        grad_gate = query_vals * grad_mid
        query_list.append((grad_mid * conv_out).astype(jnp.bfloat16))
        back_out = channel_map(long_filter, grad_gate, True)
        key_list.append((back_out * value_vals).astype(jnp.bfloat16))
        value_list.append((back_out * key_vals).astype(jnp.bfloat16))
    grad_weight = weight_total * (1.0 / math.sqrt(BATCH * SEQLEN))
    return (jnp.stack(query_list), jnp.stack(key_list), jnp.stack(value_list), grad_weight)
```

```python
import math

import jax
import jax.numpy as jnp
import ml_dtypes
import numpy as np
from jax import lax
from jax.experimental import pallas as pl
from jax.experimental.pallas import tpu as pltpu
from jax.sharding import PartitionSpec as P

WIDE = 128
TALL = 64


def split_table(values):
    high = values.astype(ml_dtypes.bfloat16)
    low = (values - high.astype(np.float64)).astype(ml_dtypes.bfloat16)
    return high, low


def make_tables(row_of):
    freq = np.arange(TALL) + 0.25
    first = 2.0 * np.pi / TALL * freq[:, None] * np.asarray(row_of)[None, :]
    first = np.concatenate([np.cos(first), -np.sin(first)], axis=0)
    high, low = split_table(first)
    analyse = np.concatenate([high, high, low], axis=1)
    last = 2.0 * np.pi / TALL * np.asarray(row_of)[:, None] * freq[None, :]
    last = np.concatenate([np.cos(last), -np.sin(last)], axis=1) / (TALL * WIDE)
    high, low = split_table(last)
    restore = np.concatenate([high, high, low], axis=1)
    return analyse, restore


def make_shared():
    freq = np.arange(TALL) + 0.25
    cols = np.arange(WIDE)
    turn = 2.0 * np.pi / (TALL * WIDE) * freq[:, None] * cols[None, :]
    twist = np.stack([np.cos(turn), np.sin(turn)]).astype(np.float32)
    angle = 2.0 * np.pi / WIDE * (cols[:, None] * cols[None, :] % WIDE)
    cos, sin = np.cos(angle), np.sin(angle)
    there = np.concatenate([np.concatenate([cos, -sin], 1), np.concatenate([sin, cos], 1)], 0)
    back = np.concatenate([np.concatenate([cos, sin], 1), np.concatenate([-sin, cos], 1)], 0)
    out = []
    for table in (there, back):
        high, low = split_table(table)
        out.append(np.concatenate([high, high, low], axis=0))
    return twist, out[0], out[1]


def halves(values):
    high = values.astype(jnp.bfloat16)
    low = (values - high.astype(jnp.float32)).astype(jnp.bfloat16)
    return high, low


def dot(left, right):
    return jnp.dot(left, right, preferred_element_type=jnp.float32)


def stacked(values):
    high, low = halves(values)
    return jnp.concatenate([high, low, high], axis=0)


def beside(values):
    high, low = halves(values)
    return jnp.concatenate([high, low, high], axis=1)


def forward_pair(pair, analyse, twist, there):
    both = dot(analyse, stacked(jnp.concatenate(pair, axis=1)))
    cos, sin = twist[0], twist[1]
    rows = []
    for which in range(2):
        real = both[:TALL, which * WIDE : (which + 1) * WIDE]
        imag = both[TALL:, which * WIDE : (which + 1) * WIDE]
        rows.append(jnp.concatenate([real * cos + imag * sin, imag * cos - real * sin], axis=1))
    return dot(beside(jnp.concatenate(rows, axis=0)), there)


def inverse_pair(spec, restore, twist, back):
    both = dot(beside(spec), back)
    cos, sin = twist[0], twist[1]
    columns = []
    for which in range(2):
        real = both[which * TALL : (which + 1) * TALL, :WIDE]
        imag = both[which * TALL : (which + 1) * TALL, WIDE:]
        columns.append(jnp.concatenate([real * cos - imag * sin, real * sin + imag * cos], axis=0))
    return dot(restore, stacked(jnp.concatenate(columns, axis=1)))


def filter_kernel(filt_ref, analyse_ref, twist_ref, there_ref, spec_ref):
    twist = twist_ref[...]
    for pair in range(filt_ref.shape[0] // 2):
        inputs = [filt_ref[2 * pair], filt_ref[2 * pair + 1]]
        spec_ref[pair] = forward_pair(inputs, analyse_ref[...], twist, there_ref[...])


def conv_kernel(conjugate, offset, signal_ref, spec_ref, analyse_ref, restore_ref, twist_ref, there_ref, back_ref, out_ref):
    twist = twist_ref[...]
    blocks, channels, width = out_ref.shape
    pieces = width // WIDE
    for pair in range(channels // 2):
        inputs = []
        for channel in (2 * pair, 2 * pair + 1):
            rows = signal_ref[:, channel, offset : offset + width]
            inputs.append(
                jnp.concatenate([rows[:, q * WIDE : (q + 1) * WIDE] for q in range(pieces)], axis=0)
            )
        spec = forward_pair(inputs, analyse_ref[...], twist, there_ref[...])
        real, imag = spec[:, :WIDE], spec[:, WIDE:]
        filt = spec_ref[pair]
        filt_real, filt_imag = filt[:, :WIDE], filt[:, WIDE:]
        if conjugate:
            filt_imag = -filt_imag
        product = jnp.concatenate(
            [real * filt_real - imag * filt_imag, real * filt_imag + imag * filt_real], axis=1
        )
        result = inverse_pair(product, restore_ref[...], twist, back_ref[...])
        for which in range(2):
            column = result[:, which * WIDE : (which + 1) * WIDE]
            row = jnp.concatenate([column[q * blocks : (q + 1) * blocks] for q in range(pieces)], axis=1)
            out_ref[:, 2 * pair + which, :] = row


def places(place_ref, step):
    chans = 8
    mine = place_ref[0]
    twin = mine + 1 - 2 * lax.rem(mine, 2)
    out = []
    for base in (mine, twin):
        for ahead in (0, chans - 2, 2):
            out.append((lax.rem(base + ahead, chans) * step, step))
        far = lax.rem(base + chans // 2, chans) * step
        out.append((far, step // 2))
        out.append((far + step // 2, step // 2))
    return out


def gate_kernel(place_ref, conv_ref, query_ref, weight_ref, *refs):
    blocks, (both_ref, mid_ref) = refs[:10], refs[10:]
    step = blocks[0].shape[0]
    total = None
    for (start, size), block in zip(places(place_ref, step), blocks):
        columns = weight_ref[:, pl.ds(pl.multiple_of(start, WIDE), size)]
        term = dot(columns, block[...])
        total = term if total is None else total + term
    mid_ref[...] = total
    seqs, rows, width = conv_ref.shape
    both_ref[:, :, :width] = conv_ref[...]
    gate = query_ref[...].astype(jnp.float32) * total
    both_ref[:, :, width:] = gate.reshape(seqs, rows, width)


def part_kernel(place_ref, both_ref, query_ref, mid_ref, *refs):
    blocks, (grad_ref, part_ref) = refs[:10], refs[10:]
    step = blocks[0].shape[0]
    channels, width = mid_ref.shape
    conv_out = both_ref[:, :, :width].reshape(channels, width)
    grad_ref[...] = (mid_ref[...] * conv_out).astype(jnp.bfloat16)
    gated = (query_ref[...].astype(jnp.float32) * conv_out).astype(jnp.bfloat16)
    for (start, size), block in zip(places(place_ref, step), blocks):
        term = lax.dot_general(
            gated, block[...], (((1,), (1,)), ((), ())), preferred_element_type=jnp.float32
        )
        part_ref[:, pl.ds(pl.multiple_of(start, WIDE), size)] = term.astype(jnp.bfloat16)


def filter_spectrum(filt, analyse, twist, there):
    channels = filt.shape[0]
    return pl.pallas_call(
        filter_kernel,
        out_shape=jax.ShapeDtypeStruct((channels // 2, 2 * TALL, 2 * WIDE), jnp.float32),
        name="filter_spectrum",
        cost_estimate=pl.CostEstimate(flops=600_000_000, bytes_accessed=2_000_000, transcendentals=0),
    )(filt, analyse, twist, there)


def convolve(signal, spec, tables, conjugate, offset, width):
    analyse, restore, twist, there, back = tables

    def kernel(*refs):
        conv_kernel(conjugate, offset, *refs)

    return pl.pallas_call(
        kernel,
        out_shape=jax.ShapeDtypeStruct(signal.shape[:2] + (width,), jnp.float32),
        name="correlate" if conjugate else "convolve",
        cost_estimate=pl.CostEstimate(flops=4_000_000_000, bytes_accessed=3_000_000, transcendentals=0),
    )(signal, spec, analyse, restore, twist, there, back)


def placed_call(kernel, name, count, out_shape):
    whole = pl.BlockSpec(memory_space=pltpu.VMEM)
    return pl.pallas_call(
        kernel,
        in_specs=[pl.BlockSpec(memory_space=pltpu.SMEM)] + [whole] * count,
        out_shape=out_shape,
        name=name,
        cost_estimate=pl.CostEstimate(flops=600_000_000, bytes_accessed=5_000_000, transcendentals=0),
    )


def gather_features(block, chans):
    def send(values, hop):
        return lax.ppermute(values, "chan", [(k, hop(k)) for k in range(chans)])

    def ahead(k):
        return (k + 2) % chans

    def behind(k):
        return (k - 2) % chans

    half = block.shape[0] // 2
    from_behind = send(block, ahead)
    from_ahead = send(block, behind)
    far_top = send(from_behind[:half], ahead)
    far_bottom = send(from_ahead[half:], behind)
    mine = [block, from_behind, from_ahead, far_top, far_bottom]
    return mine + [send(values, lambda k: k ^ 1) for values in mine]


def swap(blocks, axes="seq"):
    return lax.all_to_all(blocks, axes, split_axis=0, concat_axis=0, tiled=True)


def shards(query_proj, key_proj, value_proj, grad_out, out_weight, long_filter):
    rows, length = long_filter.shape
    seqs, chans, dps = lax.axis_size("seq"), lax.axis_size("chan"), lax.axis_size("dp")
    channels, span = query_proj.shape[1:]
    features = out_weight.shape[1]
    pieces = span // WIDE
    arrived = (np.arange(seqs)[None, :] * pieces + np.arange(pieces)[:, None]).reshape(-1)
    twist, there, back = make_shared()
    analyse_natural, _ = make_tables(np.arange(TALL))
    analyse, restore = make_tables(arrived)
    tables = tuple(jnp.asarray(t) for t in (analyse, restore, twist, there, back))
    place = lax.axis_index("chan").astype(jnp.int32).reshape(1)

    blocks = gather_features(grad_out[0], chans)
    key_vals = key_proj[0].astype(jnp.float32)
    value_vals = value_proj[0].astype(jnp.float32)
    mixed_full = swap((key_vals * value_vals).reshape(seqs, rows, span))
    spec = filter_spectrum(
        long_filter.reshape(rows, TALL, WIDE), jnp.asarray(analyse_natural), tables[2], tables[3]
    )
    conv_full = convolve(mixed_full, spec, tables, False, 0, span)

    both, grad_mid = placed_call(
        gate_kernel,
        "gate",
        13,
        (
            jax.ShapeDtypeStruct((seqs, rows, 2 * span), jnp.float32),
            jax.ShapeDtypeStruct((channels, span), jnp.float32),
        ),
    )(place, conv_full, query_proj[0], out_weight, *blocks)
    both = swap(both)
    grad_query, weight_part = placed_call(
        part_kernel,
        "part",
        13,
        (
            jax.ShapeDtypeStruct((channels, span), jnp.bfloat16),
            jax.ShapeDtypeStruct((channels, features), jnp.bfloat16),
        ),
    )(place, both, query_proj[0], grad_mid, *blocks)

    group = dps * seqs
    weight_part = swap(weight_part.reshape(group, channels // group, features), ("dp", "seq"))
    back_full = convolve(both, spec, tables, True, span, span)
    grad_mixed = swap(back_full).reshape(channels, span)
    weight_sum = jnp.sum(weight_part.astype(jnp.float32), axis=0) * (1.0 / math.sqrt(dps * length))
    copies = jnp.broadcast_to(weight_sum.astype(jnp.bfloat16)[None], (group,) + weight_sum.shape)
    grad_weight = swap(copies, ("dp", "seq")).reshape(channels, features).astype(jnp.float32)

    grad_key = (grad_mixed * value_vals).astype(jnp.bfloat16)
    grad_value = (grad_mixed * key_vals).astype(jnp.bfloat16)
    return (grad_query[None], grad_key[None], grad_value[None], grad_weight)


def solution(mesh):
    placed = (
        P("dp", "chan", "seq"),
        P("dp", "chan", "seq"),
        P("dp", "chan", "seq"),
        P("dp", "chan", "seq"),
        P("chan", None),
        P(("chan", "seq"), None),
    )
    return jax.shard_map(
        shards,
        mesh=mesh,
        in_specs=placed,
        out_specs=(
            P("dp", "chan", "seq"),
            P("dp", "chan", "seq"),
            P("dp", "chan", "seq"),
            P("chan", None),
        ),
        check_vma=False,
    )
```

```python
import math

import jax
import jax.numpy as jnp
import ml_dtypes
import numpy as np
from jax import lax
from jax.experimental import pallas as pl
from jax.experimental.pallas import tpu as pltpu
from jax.sharding import PartitionSpec as P


WIDE = 128
TALL = 64
LIMIT = 20


def split_table(values):
    high = values.astype(ml_dtypes.bfloat16)
    low = (values - high.astype(np.float64)).astype(ml_dtypes.bfloat16)
    return high, low


def make_tables(row_of):
    freq = np.arange(TALL) + 0.25
    first = 2.0 * np.pi / TALL * freq[:, None] * np.asarray(row_of)[None, :]
    first = np.concatenate([np.cos(first), -np.sin(first)], axis=0)
    high, low = split_table(first)
    analyse = np.concatenate([high, high, low], axis=1)
    last = 2.0 * np.pi / TALL * np.asarray(row_of)[:, None] * freq[None, :]
    last = np.concatenate([np.cos(last), -np.sin(last)], axis=1) / (TALL * WIDE)
    high, low = split_table(last)
    restore = np.concatenate([high, high, low], axis=1)
    return analyse, restore


def make_shared():
    freq = np.arange(TALL) + 0.25
    cols = np.arange(WIDE)
    turn = 2.0 * np.pi / (TALL * WIDE) * freq[:, None] * cols[None, :]
    twist = np.stack([np.cos(turn), np.sin(turn)]).astype(np.float32)
    angle = 2.0 * np.pi / WIDE * (cols[:, None] * cols[None, :] % WIDE)
    cos, sin = np.cos(angle), np.sin(angle)
    there = np.concatenate([np.concatenate([cos, -sin], 1), np.concatenate([sin, cos], 1)], 0)
    back = np.concatenate([np.concatenate([cos, sin], 1), np.concatenate([-sin, cos], 1)], 0)
    out = []
    for table in (there, back):
        high, low = split_table(table)
        out.append(np.concatenate([high, high, low], axis=0))
    return twist, out[0], out[1]


def halves(values):
    high = values.astype(jnp.bfloat16)
    low = (values - high.astype(jnp.float32)).astype(jnp.bfloat16)
    return high, low


def dot(left, right):
    return jnp.dot(left, right, preferred_element_type=jnp.float32)


def stacked(values):
    high, low = halves(values)
    return jnp.concatenate([high, low, high], axis=0)


def beside(values):
    high, low = halves(values)
    return jnp.concatenate([high, low, high], axis=1)


def forward_pair(pair, analyse, twist, there):
    both = dot(analyse, stacked(jnp.concatenate(pair, axis=1)))
    cos, sin = twist[0], twist[1]
    rows = []
    for which in range(2):
        real = both[:TALL, which * WIDE : (which + 1) * WIDE]
        imag = both[TALL:, which * WIDE : (which + 1) * WIDE]
        rows.append(jnp.concatenate([real * cos + imag * sin, imag * cos - real * sin], axis=1))
    return dot(beside(jnp.concatenate(rows, axis=0)), there)


def inverse_pair(spec, restore, twist, back):
    both = dot(beside(spec), back)
    cos, sin = twist[0], twist[1]
    columns = []
    for which in range(2):
        real = both[which * TALL : (which + 1) * TALL, :WIDE]
        imag = both[which * TALL : (which + 1) * TALL, WIDE:]
        columns.append(jnp.concatenate([real * cos - imag * sin, real * sin + imag * cos], axis=0))
    return dot(restore, stacked(jnp.concatenate(columns, axis=1)))


def filter_kernel(filt_ref, analyse_ref, twist_ref, there_ref, spec_ref):
    twist = twist_ref[...]
    for pair in range(filt_ref.shape[0] // 2):
        inputs = [filt_ref[2 * pair], filt_ref[2 * pair + 1]]
        spec_ref[pair] = forward_pair(inputs, analyse_ref[...], twist, there_ref[...])


def conv_kernel(conjugate, offset, signal_ref, spec_ref, analyse_ref, restore_ref, twist_ref, there_ref, back_ref, out_ref):
    twist = twist_ref[...]
    blocks, channels, width = out_ref.shape
    pieces = width // WIDE
    for pair in range(channels // 2):
        inputs = []
        for channel in (2 * pair, 2 * pair + 1):
            rows = signal_ref[:, channel, offset : offset + width]
            inputs.append(
                jnp.concatenate([rows[:, q * WIDE : (q + 1) * WIDE] for q in range(pieces)], axis=0)
            )
        spec = forward_pair(inputs, analyse_ref[...], twist, there_ref[...])
        real, imag = spec[:, :WIDE], spec[:, WIDE:]
        filt = spec_ref[pair]
        filt_real, filt_imag = filt[:, :WIDE], filt[:, WIDE:]
        if conjugate:
            filt_imag = -filt_imag
        product = jnp.concatenate(
            [real * filt_real - imag * filt_imag, real * filt_imag + imag * filt_real], axis=1
        )
        result = inverse_pair(product, restore_ref[...], twist, back_ref[...])
        for which in range(2):
            column = result[:, which * WIDE : (which + 1) * WIDE]
            row = jnp.concatenate([column[q * blocks : (q + 1) * blocks] for q in range(pieces)], axis=1)
            out_ref[:, 2 * pair + which, :] = row


def places(place_ref, step):
    chans = 8
    mine = place_ref[0]
    twin = mine + 1 - 2 * lax.rem(mine, 2)
    out = []
    for base in (mine, twin):
        for ahead in (0, chans - 2, 2):
            out.append((lax.rem(base + ahead, chans) * step, step))
        far = lax.rem(base + chans // 2, chans) * step
        out.append((far, step // 2))
        out.append((far + step // 2, step // 2))
    return out


def gate_kernel(place_ref, conv_ref, query_ref, weight_ref, *refs):
    blocks, (both_ref, mid_ref) = refs[:10], refs[10:]
    step = blocks[0].shape[0]
    total = None
    for (start, size), block in zip(places(place_ref, step), blocks):
        columns = weight_ref[:, pl.ds(pl.multiple_of(start, WIDE), size)]
        term = dot(columns, block[...])
        total = term if total is None else total + term
    mid_ref[...] = total
    seqs, rows, width = conv_ref.shape
    both_ref[:, :, :width] = conv_ref[...]
    gate = query_ref[...].astype(jnp.float32) * total
    both_ref[:, :, width:] = gate.reshape(seqs, rows, width)


def part_kernel(place_ref, both_ref, query_ref, *refs):
    blocks, (part_ref,) = refs[:10], refs[10:]
    step = blocks[0].shape[0]
    channels, width = query_ref.shape
    conv_out = both_ref[:, :, :width].reshape(channels, width)
    gated = (query_ref[...].astype(jnp.float32) * conv_out).astype(jnp.bfloat16)
    for (start, size), block in zip(places(place_ref, step), blocks):
        term = lax.dot_general(
            gated, block[...], (((1,), (1,)), ((), ())), preferred_element_type=jnp.float32
        )
        part_ref[:, pl.ds(pl.multiple_of(start, WIDE), size)] = term.astype(jnp.bfloat16)


def total_kernel(scale, part_ref, out_ref):
    group, rows, features = part_ref.shape
    half = features // 2
    total = part_ref[0].astype(jnp.float32)
    for source in range(1, group):
        total = total + part_ref[source].astype(jnp.float32)
    total = (total * scale).astype(jnp.bfloat16)
    out_ref[:rows, :] = total[:, :half]
    out_ref[rows:, :] = total[:, half:]


def last_kernel(mine_ref, other_ref, back_ref, out_ref):
    seqs, _, span = back_ref.shape
    rows = mine_ref.shape[0]
    for target in range(seqs):
        out_ref[target, :rows, :] = mine_ref[...]
        out_ref[target, rows : 2 * rows, :] = other_ref[...]
        high, low = halves(back_ref[target])
        out_ref[target, 2 * rows :, :span] = high
        out_ref[target, 2 * rows :, span:] = low


def final_kernel(dp_ref, all_ref, key_ref, value_ref, grad_key_ref, grad_value_ref, grad_weight_ref):
    seqs, _, half = all_ref.shape
    channels, span = key_ref.shape
    rows = channels // (2 * seqs)
    lanes = channels // seqs
    for source in range(seqs):
        for turn in range(2):
            owner = dp_ref[0] + turn - 2 * turn * dp_ref[0]
            place = pl.ds(pl.multiple_of(owner * (channels // 2) + source * rows, 8), rows)
            piece = all_ref[source, 2 * turn * rows : 2 * (turn + 1) * rows, :].astype(jnp.float32)
            grad_weight_ref[place, :half] = piece[:rows]
            grad_weight_ref[place, half:] = piece[rows:]
        both = all_ref[source, 4 * rows :, :].astype(jnp.float32)
        mixed = both[:, :span] + both[:, span:]
        place = slice(source * lanes, (source + 1) * lanes)
        grad_key_ref[place, :] = (mixed * value_ref[place, :].astype(jnp.float32)).astype(jnp.bfloat16)
        grad_value_ref[place, :] = (mixed * key_ref[place, :].astype(jnp.float32)).astype(jnp.bfloat16)


def limited(mebibytes):
    return pltpu.CompilerParams(vmem_limit_bytes=mebibytes * 1024 * 1024)


def filter_spectrum(filt, analyse, twist, there):
    channels = filt.shape[0]
    return pl.pallas_call(
        filter_kernel,
        out_shape=jax.ShapeDtypeStruct((channels // 2, 2 * TALL, 2 * WIDE), jnp.float32),
        name="filter_spectrum",
        cost_estimate=pl.CostEstimate(flops=600_000_000, bytes_accessed=2_000_000, transcendentals=0),
    )(filt, analyse, twist, there)


def convolve(signal, spec, tables, conjugate, offset, width):
    analyse, restore, twist, there, back = tables

    def kernel(*refs):
        conv_kernel(conjugate, offset, *refs)

    return pl.pallas_call(
        kernel,
        out_shape=jax.ShapeDtypeStruct(signal.shape[:2] + (width,), jnp.float32),
        name="correlate" if conjugate else "convolve",
        cost_estimate=pl.CostEstimate(flops=4_000_000_000, bytes_accessed=3_000_000, transcendentals=0),
    )(signal, spec, analyse, restore, twist, there, back)


def placed_call(kernel, count, out_shape):
    whole = pl.BlockSpec(memory_space=pltpu.VMEM)
    return pl.pallas_call(
        kernel,
        in_specs=[pl.BlockSpec(memory_space=pltpu.SMEM)] + [whole] * count,
        out_shape=out_shape,
        compiler_params=limited(LIMIT),
        cost_estimate=pl.CostEstimate(flops=600_000_000, bytes_accessed=5_000_000, transcendentals=0),
    )


def gather_features(block, chans):
    def send(values, hop):
        return lax.ppermute(values, "chan", [(k, hop(k)) for k in range(chans)])

    def ahead(k):
        return (k + 2) % chans

    def behind(k):
        return (k - 2) % chans

    half = block.shape[0] // 2
    from_behind = send(block, ahead)
    from_ahead = send(block, behind)
    far_top = send(from_behind[:half], ahead)
    far_bottom = send(from_ahead[half:], behind)
    mine = [block, from_behind, from_ahead, far_top, far_bottom]
    return mine + [send(values, lambda k: k ^ 1) for values in mine]


def swap(blocks, axes="seq"):
    return lax.all_to_all(blocks, axes, split_axis=0, concat_axis=0, tiled=True)


def shards(query_proj, key_proj, value_proj, grad_out, out_weight, long_filter):
    rows, length = long_filter.shape
    seqs, chans, dps = lax.axis_size("seq"), lax.axis_size("chan"), lax.axis_size("dp")
    channels, span = query_proj.shape[1:]
    features = out_weight.shape[1]
    pieces = span // WIDE
    arrived = (np.arange(seqs)[None, :] * pieces + np.arange(pieces)[:, None]).reshape(-1)
    twist, there, back = make_shared()
    analyse_natural, _ = make_tables(np.arange(TALL))
    analyse, restore = make_tables(arrived)
    tables = tuple(jnp.asarray(t) for t in (analyse, restore, twist, there, back))
    place = lax.axis_index("chan").astype(jnp.int32).reshape(1)

    blocks = gather_features(grad_out[0], chans)
    key_vals = key_proj[0].astype(jnp.float32)
    value_vals = value_proj[0].astype(jnp.float32)
    mixed_full = swap((key_vals * value_vals).reshape(seqs, rows, span))
    spec = filter_spectrum(long_filter.reshape(rows, TALL, WIDE), jnp.asarray(analyse_natural), tables[2], tables[3])
    conv_full = convolve(mixed_full, spec, tables, False, 0, span)

    both, grad_mid = placed_call(
        gate_kernel,
        13,
        (
            jax.ShapeDtypeStruct((seqs, rows, 2 * span), jnp.float32),
            jax.ShapeDtypeStruct((channels, span), jnp.float32),
        ),
    )(place, conv_full, query_proj[0], out_weight, *blocks)
    both = swap(both)
    weight_part = placed_call(
        part_kernel, 12, jax.ShapeDtypeStruct((channels, features), jnp.bfloat16)
    )(place, both, query_proj[0], *blocks)
    grad_query = (grad_mid * both[:, :, :span].reshape(channels, span)).astype(jnp.bfloat16)

    group = dps * seqs
    weight_part = swap(weight_part.reshape(group, channels // group, features), ("dp", "seq"))
    back_full = convolve(both, spec, tables, True, span, span)
    scale = 1.0 / math.sqrt(dps * length)
    half = features // 2
    mine = pl.pallas_call(
        lambda *refs: total_kernel(scale, *refs),
        out_shape=jax.ShapeDtypeStruct((2 * (channels // group), half), jnp.bfloat16),
        name="total",
        compiler_params=limited(LIMIT),
    )(weight_part)
    other = lax.ppermute(mine, "dp", [(0, 1), (1, 0)])
    last = pl.pallas_call(
        last_kernel,
        out_shape=jax.ShapeDtypeStruct((seqs, 4 * (channels // group) + rows, half), jnp.bfloat16),
        name="last",
        compiler_params=limited(LIMIT),
    )(mine, other, back_full)
    last = swap(last)
    grad_key, grad_value, grad_weight = placed_call(
        final_kernel,
        3,
        (
            jax.ShapeDtypeStruct((channels, span), jnp.bfloat16),
            jax.ShapeDtypeStruct((channels, span), jnp.bfloat16),
            jax.ShapeDtypeStruct((channels, features), jnp.float32),
        ),
    )(lax.axis_index("dp").astype(jnp.int32).reshape(1), last, key_proj[0], value_proj[0])
    return (grad_query[None], grad_key[None], grad_value[None], grad_weight)


def solution(mesh):
    placed = (
        P("dp", "chan", "seq"),
        P("dp", "chan", "seq"),
        P("dp", "chan", "seq"),
        P("dp", "chan", "seq"),
        P("chan", None),
        P(("chan", "seq"), None),
    )
    return jax.shard_map(
        shards,
        mesh=mesh,
        in_specs=placed,
        out_specs=(
            P("dp", "chan", "seq"),
            P("dp", "chan", "seq"),
            P("dp", "chan", "seq"),
            P("chan", None),
        ),
        check_vma=False,
    )
```

```python
import math

import jax
import jax.numpy as jnp
import ml_dtypes
import numpy as np
from jax import lax
from jax.experimental import pallas as pl
from jax.experimental.pallas import tpu as pltpu
from jax.sharding import PartitionSpec as P


WIDE = 128
TALL = 64
LIMIT = 20
BATCH = 8


def split_table(values):
    high = values.astype(ml_dtypes.bfloat16)
    low = (values - high.astype(np.float64)).astype(ml_dtypes.bfloat16)
    return high, low


def make_tables(row_of):
    freq = np.arange(TALL) + 0.25
    first = 2.0 * np.pi / TALL * freq[:, None] * np.asarray(row_of)[None, :]
    first = np.concatenate([np.cos(first), -np.sin(first)], axis=0)
    high, low = split_table(first)
    analyse = np.concatenate([high, high, low], axis=1)
    last = 2.0 * np.pi / TALL * np.asarray(row_of)[:, None] * freq[None, :]
    last = np.concatenate([np.cos(last), -np.sin(last)], axis=1) / (TALL * WIDE)
    high, low = split_table(last)
    restore = np.concatenate([high, high, low], axis=1)
    return analyse, restore


def make_shared():
    freq = np.arange(TALL) + 0.25
    cols = np.arange(WIDE)
    turn = 2.0 * np.pi / (TALL * WIDE) * freq[:, None] * cols[None, :]
    twist = np.stack([np.cos(turn), np.sin(turn)]).astype(np.float32)
    angle = 2.0 * np.pi / WIDE * (cols[:, None] * cols[None, :] % WIDE)
    cos, sin = np.cos(angle), np.sin(angle)
    there = np.concatenate([np.concatenate([cos, -sin], 1), np.concatenate([sin, cos], 1)], 0)
    back = np.concatenate([np.concatenate([cos, sin], 1), np.concatenate([-sin, cos], 1)], 0)
    out = []
    for table in (there, back):
        high, low = split_table(table)
        out.append(np.concatenate([high, high, low], axis=0))
    return twist, out[0], out[1]


def halves(values):
    high = values.astype(jnp.bfloat16)
    low = (values - high.astype(jnp.float32)).astype(jnp.bfloat16)
    return high, low


def dot(left, right):
    return jnp.dot(left, right, preferred_element_type=jnp.float32)


def stacked(values):
    high, low = halves(values)
    return jnp.concatenate([high, low, high], axis=0)


def beside(values):
    high, low = halves(values)
    return jnp.concatenate([high, low, high], axis=1)


def forward_group(inputs, analyse, twist, there):
    both = dot(analyse, stacked(jnp.concatenate(inputs, axis=1)))
    cos, sin = twist[0], twist[1]
    rows = []
    for which in range(len(inputs)):
        real = both[:TALL, which * WIDE : (which + 1) * WIDE]
        imag = both[TALL:, which * WIDE : (which + 1) * WIDE]
        rows.append(jnp.concatenate([real * cos + imag * sin, imag * cos - real * sin], axis=1))
    return dot(beside(jnp.concatenate(rows, axis=0)), there)


def inverse_group(spec, restore, twist, back):
    both = dot(beside(spec), back)
    cos, sin = twist[0], twist[1]
    columns = []
    for which in range(spec.shape[0] // TALL):
        real = both[which * TALL : (which + 1) * TALL, :WIDE]
        imag = both[which * TALL : (which + 1) * TALL, WIDE:]
        columns.append(jnp.concatenate([real * cos - imag * sin, real * sin + imag * cos], axis=0))
    return dot(restore, stacked(jnp.concatenate(columns, axis=1)))


def product(left, right, conjugate):
    real, imag = left[:, :WIDE], left[:, WIDE:]
    other_real, other_imag = right[:, :WIDE], right[:, WIDE:]
    if conjugate:
        other_imag = -other_imag
    return jnp.concatenate(
        [real * other_real - imag * other_imag, real * other_imag + imag * other_real], axis=1
    )


def arrived_rows(signal_ref, channel, offset, width):
    rows = signal_ref[:, channel, offset : offset + width]
    return jnp.concatenate([rows[:, q * WIDE : (q + 1) * WIDE] for q in range(width // WIDE)], axis=0)


def sent_rows(result, which, blocks):
    column = result[:, which * WIDE : (which + 1) * WIDE]
    return jnp.concatenate(
        [column[q * blocks : (q + 1) * blocks] for q in range(TALL // blocks)], axis=1
    )


def convolve_kernel(signal_ref, filt_ref, natural_ref, analyse_ref, restore_ref, twist_ref, there_ref, back_ref, out_ref, spec_ref, rows_ref):
    twist = twist_ref[...]
    blocks, channels, width = out_ref.shape
    for place in range(TALL):
        rows_ref[place] = filt_ref[:, place * WIDE : (place + 1) * WIDE]
    for group in range(channels // BATCH):
        members = range(group * BATCH, (group + 1) * BATCH)
        filt = forward_group([rows_ref[:, m, :] for m in members], natural_ref[...], twist, there_ref[...])
        spec_ref[group] = filt
        inputs = [arrived_rows(signal_ref, m, 0, width) for m in members]
        spec = forward_group(inputs, analyse_ref[...], twist, there_ref[...])
        result = inverse_group(product(spec, filt, False), restore_ref[...], twist, back_ref[...])
        for which, m in enumerate(members):
            out_ref[:, m, :] = sent_rows(result, which, blocks)


def correlate_kernel(signal_ref, spec_ref, analyse_ref, restore_ref, twist_ref, there_ref, back_ref, out_ref, rows_ref):
    twist = twist_ref[...]
    blocks, channels, width = rows_ref.shape
    below = out_ref.shape[1] - channels
    for group in range(channels // BATCH):
        members = range(group * BATCH, (group + 1) * BATCH)
        inputs = [arrived_rows(signal_ref, m, width, width) for m in members]
        spec = forward_group(inputs, analyse_ref[...], twist, there_ref[...])
        result = inverse_group(product(spec, spec_ref[group], True), restore_ref[...], twist, back_ref[...])
        for which, m in enumerate(members):
            rows_ref[:, m, :] = sent_rows(result, which, blocks)
    high, low = halves(rows_ref[...])
    out_ref[:, below:, :width] = high
    out_ref[:, below:, width:] = low


def places(place_ref, step):
    chans = 8
    mine = place_ref[0]
    twin = mine + 1 - 2 * lax.rem(mine, 2)
    out = []
    for base in (mine, twin):
        for ahead in (0, chans - 2, 2):
            out.append((lax.rem(base + ahead, chans) * step, step))
        far = lax.rem(base + chans // 2, chans) * step
        out.append((far, step // 2))
        out.append((far + step // 2, step // 2))
    return out


def mix_kernel(key_ref, value_ref, out_ref):
    mixed = key_ref[...].astype(jnp.float32) * value_ref[...].astype(jnp.float32)
    out_ref[...] = mixed.reshape(out_ref.shape)


def gate_kernel(place_ref, conv_ref, query_ref, weight_ref, *refs):
    blocks, (both_ref, mid_ref, sem) = refs[:10], refs[10:]
    step = blocks[0].shape[0]
    seqs, rows, width = conv_ref.shape
    copy = pltpu.make_async_copy(conv_ref, both_ref.at[:, :, :width], sem)
    copy.start()
    total = None
    for (start, size), block in zip(places(place_ref, step), blocks):
        columns = weight_ref[:, pl.ds(pl.multiple_of(start, WIDE), size)]
        term = dot(columns, block[...])
        total = term if total is None else total + term
    mid_ref[...] = total
    gate = query_ref[...].astype(jnp.float32) * total
    both_ref[:, :, width:] = gate.reshape(seqs, rows, width)
    copy.wait()


def part_kernel(place_ref, both_ref, query_ref, *refs):
    blocks, (part_ref,) = refs[:10], refs[10:]
    step = blocks[0].shape[0]
    channels, width = query_ref.shape
    conv_out = both_ref[:, :, :width].reshape(channels, width)
    gated = (query_ref[...].astype(jnp.float32) * conv_out).astype(jnp.bfloat16)
    for (start, size), block in zip(places(place_ref, step), blocks):
        term = lax.dot_general(
            gated, block[...], (((1,), (1,)), ((), ())), preferred_element_type=jnp.float32
        )
        part_ref[:, pl.ds(pl.multiple_of(start, WIDE), size)] = term.astype(jnp.bfloat16)


def total_kernel(scale, part_ref, out_ref):
    group, rows, features = part_ref.shape
    half = features // 2
    total = part_ref[0].astype(jnp.float32)
    for source in range(1, group):
        total = total + part_ref[source].astype(jnp.float32)
    total = (total * scale).astype(jnp.bfloat16)
    out_ref[:rows, :] = total[:, :half]
    out_ref[rows:, :] = total[:, half:]


def last_kernel(mine_ref, other_ref, back_ref, out_ref, sems):
    rows = mine_ref.shape[0]
    copies = []
    for target in range(out_ref.shape[0]):
        for turn, source in enumerate((mine_ref, other_ref)):
            place = out_ref.at[target, turn * rows : (turn + 1) * rows, :]
            copies.append(pltpu.make_async_copy(source, place, sems.at[target, turn]))
    for copy in copies:
        copy.start()
    for copy in copies:
        copy.wait()


def final_kernel(dp_ref, all_ref, key_ref, value_ref, grad_key_ref, grad_value_ref, grad_weight_ref):
    seqs, _, half = all_ref.shape
    channels, span = key_ref.shape
    rows = channels // (2 * seqs)
    lanes = channels // seqs
    for source in range(seqs):
        for turn in range(2):
            owner = dp_ref[0] + turn - 2 * turn * dp_ref[0]
            place = pl.ds(pl.multiple_of(owner * (channels // 2) + source * rows, 8), rows)
            piece = all_ref[source, 2 * turn * rows : 2 * (turn + 1) * rows, :].astype(jnp.float32)
            grad_weight_ref[place, :half] = piece[:rows]
            grad_weight_ref[place, half:] = piece[rows:]
        both = all_ref[source, 4 * rows :, :].astype(jnp.float32)
        mixed = both[:, :span] + both[:, span:]
        place = slice(source * lanes, (source + 1) * lanes)
        grad_key_ref[place, :] = (mixed * value_ref[place, :].astype(jnp.float32)).astype(jnp.bfloat16)
        grad_value_ref[place, :] = (mixed * key_ref[place, :].astype(jnp.float32)).astype(jnp.bfloat16)


def limited(mebibytes):
    return pltpu.CompilerParams(vmem_limit_bytes=mebibytes * 1024 * 1024)


def convolve(signal, filt, natural, tables):
    _, channels, _ = signal.shape
    return pl.pallas_call(
        convolve_kernel,
        out_shape=(
            jax.ShapeDtypeStruct(signal.shape, jnp.float32),
            jax.ShapeDtypeStruct((channels // BATCH, BATCH * TALL, 2 * WIDE), jnp.float32),
        ),
        scratch_shapes=[pltpu.VMEM((TALL, channels, WIDE), jnp.float32)],
        name="convolve",
        cost_estimate=pl.CostEstimate(flops=4_000_000_000, bytes_accessed=3_000_000, transcendentals=0),
    )(signal, filt, natural, *tables)


def correlate(both, spec, tables, above):
    blocks, channels, double = both.shape
    return pl.pallas_call(
        correlate_kernel,
        out_shape=jax.ShapeDtypeStruct((blocks, above + channels, double), jnp.bfloat16),
        scratch_shapes=[pltpu.VMEM((blocks, channels, double // 2), jnp.float32)],
        name="correlate",
        cost_estimate=pl.CostEstimate(flops=4_000_000_000, bytes_accessed=3_000_000, transcendentals=0),
    )(both, spec, *tables)


def placed_call(kernel, count, out_shape, left=()):
    whole = pl.BlockSpec(memory_space=pltpu.VMEM)
    return pl.pallas_call(
        kernel,
        in_specs=[pl.BlockSpec(memory_space=pltpu.SMEM)]
        + [pl.BlockSpec(memory_space=pltpu.HBM)] * len(left)
        + [whole] * (count - len(left)),
        scratch_shapes=[pltpu.SemaphoreType.DMA] * len(left),
        out_shape=out_shape,
        compiler_params=limited(LIMIT),
        cost_estimate=pl.CostEstimate(flops=600_000_000, bytes_accessed=5_000_000, transcendentals=0),
    )


def gather_features(block, chans):
    def send(values, hop):
        return lax.ppermute(values, "chan", [(k, hop(k)) for k in range(chans)])

    def ahead(k):
        return (k + 2) % chans

    def behind(k):
        return (k - 2) % chans

    half = block.shape[0] // 2
    from_behind = send(block, ahead)
    from_ahead = send(block, behind)
    far_top = send(from_behind[:half], ahead)
    far_bottom = send(from_ahead[half:], behind)
    mine = [block, from_behind, from_ahead, far_top, far_bottom]
    return mine + [send(values, lambda k: k ^ 1) for values in mine]


def swap(blocks, axes="seq"):
    return lax.all_to_all(blocks, axes, split_axis=0, concat_axis=0, tiled=True)


def shards(query_proj, key_proj, value_proj, grad_out, out_weight, long_filter):
    rows, length = long_filter.shape
    seqs, chans, dps = lax.axis_size("seq"), lax.axis_size("chan"), lax.axis_size("dp")
    channels, span = query_proj.shape[1:]
    features = out_weight.shape[1]
    pieces = span // WIDE
    arrived = (np.arange(seqs)[None, :] * pieces + np.arange(pieces)[:, None]).reshape(-1)
    twist, there, back = make_shared()
    analyse_natural, _ = make_tables(np.arange(TALL))
    analyse, restore = make_tables(arrived)
    tables = tuple(jnp.asarray(t) for t in (analyse, restore, twist, there, back))
    place = lax.axis_index("chan").astype(jnp.int32).reshape(1)

    blocks = gather_features(grad_out[0], chans)
    mixed_in = pl.pallas_call(
        mix_kernel,
        out_shape=jax.ShapeDtypeStruct((seqs, rows, span), jnp.float32),
        name="mix",
    )(key_proj[0], value_proj[0])
    mixed_full = swap(mixed_in)
    conv_full, spec = convolve(mixed_full, long_filter, jnp.asarray(analyse_natural), tables)

    both, grad_mid = placed_call(
        gate_kernel,
        13,
        (
            jax.ShapeDtypeStruct((seqs, rows, 2 * span), jnp.float32),
            jax.ShapeDtypeStruct((channels, span), jnp.float32),
        ),
        left=(0,),
    )(place, pltpu.with_memory_space_constraint(conv_full, pltpu.HBM), query_proj[0], out_weight, *blocks)
    both = swap(both)
    weight_part = placed_call(
        part_kernel, 12, jax.ShapeDtypeStruct((channels, features), jnp.bfloat16)
    )(place, both, query_proj[0], *blocks)
    grad_query = (grad_mid * both[:, :, :span].reshape(channels, span)).astype(jnp.bfloat16)

    group = dps * seqs
    weight_part = swap(weight_part.reshape(group, channels // group, features), ("dp", "seq"))
    back_full = correlate(both, spec, tables, 4 * (channels // group))
    scale = 1.0 / math.sqrt(dps * length)
    half = features // 2
    mine = pl.pallas_call(
        lambda *refs: total_kernel(scale, *refs),
        out_shape=jax.ShapeDtypeStruct((2 * (channels // group), half), jnp.bfloat16),
        name="total",
        compiler_params=limited(LIMIT),
    )(weight_part)
    other = lax.ppermute(mine, "dp", [(0, 1), (1, 0)])
    whole = pl.BlockSpec(memory_space=pltpu.VMEM)
    left = pl.BlockSpec(memory_space=pltpu.HBM)
    last = pl.pallas_call(
        last_kernel,
        in_specs=[whole, whole, left],
        out_specs=left,
        out_shape=jax.ShapeDtypeStruct(back_full.shape, back_full.dtype),
        input_output_aliases={2: 0},
        scratch_shapes=[pltpu.SemaphoreType.DMA((seqs, 2))],
        name="last",
        compiler_params=limited(LIMIT),
    )(mine, other, pltpu.with_memory_space_constraint(back_full, pltpu.HBM))
    last = swap(last)
    grad_key, grad_value, grad_weight = placed_call(
        final_kernel,
        3,
        (
            jax.ShapeDtypeStruct((channels, span), jnp.bfloat16),
            jax.ShapeDtypeStruct((channels, span), jnp.bfloat16),
            jax.ShapeDtypeStruct((channels, features), jnp.float32),
        ),
    )(lax.axis_index("dp").astype(jnp.int32).reshape(1), last, key_proj[0], value_proj[0])
    return (grad_query[None], grad_key[None], grad_value[None], grad_weight)


def solution(mesh):
    placed = (
        P("dp", "chan", "seq"),
        P("dp", "chan", "seq"),
        P("dp", "chan", "seq"),
        P("dp", "chan", "seq"),
        P("chan", None),
        P(("chan", "seq"), None),
    )
    return jax.shard_map(
        shards,
        mesh=mesh,
        in_specs=placed,
        out_specs=(
            P("dp", "chan", "seq"),
            P("dp", "chan", "seq"),
            P("dp", "chan", "seq"),
            P("chan", None),
        ),
        check_vma=False,
    )
```

```python
import math

import jax
import jax.numpy as jnp
import ml_dtypes
import numpy as np
from jax import lax
from jax.experimental import pallas as pl
from jax.experimental.pallas import tpu as pltpu
from jax.sharding import PartitionSpec as P


WIDE = 128
TALL = 64
LIMIT = 20
BATCH = 16


def split_table(values):
    high = values.astype(ml_dtypes.bfloat16)
    low = (values - high.astype(np.float64)).astype(ml_dtypes.bfloat16)
    return high, low


def make_tables(row_of):
    freq = np.arange(TALL) + 0.25
    first = 2.0 * np.pi / TALL * freq[:, None] * np.asarray(row_of)[None, :]
    first = np.concatenate([np.cos(first), -np.sin(first)], axis=0)
    high, low = split_table(first)
    analyse = np.concatenate([high, high, low], axis=1)
    last = 2.0 * np.pi / TALL * np.asarray(row_of)[:, None] * freq[None, :]
    last = np.concatenate([np.cos(last), -np.sin(last)], axis=1) / (TALL * WIDE)
    high, low = split_table(last)
    restore = np.concatenate([high, high, low], axis=1)
    return analyse, restore


def make_shared():
    freq = np.arange(TALL) + 0.25
    cols = np.arange(WIDE)
    turn = 2.0 * np.pi / (TALL * WIDE) * freq[:, None] * cols[None, :]
    twist = np.stack([np.cos(turn), np.sin(turn)]).astype(np.float32)
    angle = 2.0 * np.pi / WIDE * (cols[:, None] * cols[None, :] % WIDE)
    cos, sin = np.cos(angle), np.sin(angle)
    there = np.concatenate([np.concatenate([cos, -sin], 1), np.concatenate([sin, cos], 1)], 0)
    back = np.concatenate([np.concatenate([cos, sin], 1), np.concatenate([-sin, cos], 1)], 0)
    out = []
    for table in (there, back):
        high, low = split_table(table)
        out.append(np.concatenate([high, high, low], axis=0))
    return twist, out[0], out[1]


def halves(values):
    high = values.astype(jnp.bfloat16)
    low = (values - high.astype(jnp.float32)).astype(jnp.bfloat16)
    return high, low


def dot(left, right):
    return jnp.dot(left, right, preferred_element_type=jnp.float32)


def stacked(values):
    high, low = halves(values)
    return jnp.concatenate([high, low, high], axis=0)


def beside(values):
    high, low = halves(values)
    return jnp.concatenate([high, low, high], axis=1)


def forward_group(inputs, analyse, twist, there):
    both = dot(analyse, stacked(jnp.concatenate(inputs, axis=1)))
    cos, sin = twist[0], twist[1]
    rows = []
    for which in range(len(inputs)):
        real = both[:TALL, which * WIDE : (which + 1) * WIDE]
        imag = both[TALL:, which * WIDE : (which + 1) * WIDE]
        rows.append(jnp.concatenate([real * cos + imag * sin, imag * cos - real * sin], axis=1))
    return dot(beside(jnp.concatenate(rows, axis=0)), there)


def inverse_group(spec, restore, twist, back):
    both = dot(beside(spec), back)
    cos, sin = twist[0], twist[1]
    columns = []
    for which in range(spec.shape[0] // TALL):
        real = both[which * TALL : (which + 1) * TALL, :WIDE]
        imag = both[which * TALL : (which + 1) * TALL, WIDE:]
        columns.append(jnp.concatenate([real * cos - imag * sin, real * sin + imag * cos], axis=0))
    return dot(restore, stacked(jnp.concatenate(columns, axis=1)))


def product(left, right, conjugate):
    real, imag = left[:, :WIDE], left[:, WIDE:]
    other_real, other_imag = right[:, :WIDE], right[:, WIDE:]
    if conjugate:
        other_imag = -other_imag
    return jnp.concatenate(
        [real * other_real - imag * other_imag, real * other_imag + imag * other_real], axis=1
    )


def arrived_rows(signal_ref, channel, offset, width):
    rows = signal_ref[:, channel, offset : offset + width]
    return jnp.concatenate([rows[:, q * WIDE : (q + 1) * WIDE] for q in range(width // WIDE)], axis=0)


def sent_rows(result, which, blocks):
    column = result[:, which * WIDE : (which + 1) * WIDE]
    return jnp.concatenate(
        [column[q * blocks : (q + 1) * blocks] for q in range(TALL // blocks)], axis=1
    )


def convolve_kernel(signal_ref, filt_ref, natural_ref, analyse_ref, restore_ref, twist_ref, there_ref, back_ref, out_ref, spec_ref, taps_ref, rows_ref):
    twist = twist_ref[...]
    blocks, channels, width = signal_ref.shape
    for place in range(TALL):
        taps_ref[place] = filt_ref[:, place * WIDE : (place + 1) * WIDE]
    for group in range(channels // BATCH):
        members = range(group * BATCH, (group + 1) * BATCH)
        filt = forward_group([taps_ref[:, m, :] for m in members], natural_ref[...], twist, there_ref[...])
        spec_ref[group] = filt
        inputs = [arrived_rows(signal_ref, m, 0, width) for m in members]
        spec = forward_group(inputs, analyse_ref[...], twist, there_ref[...])
        result = inverse_group(product(spec, filt, False), restore_ref[...], twist, back_ref[...])
        for which, m in enumerate(members):
            rows_ref[:, m, :] = sent_rows(result, which, blocks)
    high, low = halves(rows_ref[...])
    out_ref[:, :, :width] = high
    out_ref[:, :, width:] = low


def correlate_kernel(both_ref, spec_ref, analyse_ref, restore_ref, twist_ref, there_ref, back_ref, out_ref, signal_ref, rows_ref):
    twist = twist_ref[...]
    blocks, channels, width = rows_ref.shape
    below = out_ref.shape[1] - channels
    signal_ref[...] = both_ref[:, :, 2 * width :].astype(jnp.float32)
    for group in range(channels // BATCH):
        members = range(group * BATCH, (group + 1) * BATCH)
        inputs = [arrived_rows(signal_ref, m, 0, width) for m in members]
        spec = forward_group(inputs, analyse_ref[...], twist, there_ref[...])
        result = inverse_group(product(spec, spec_ref[group], True), restore_ref[...], twist, back_ref[...])
        for which, m in enumerate(members):
            rows_ref[:, m, :] = sent_rows(result, which, blocks)
    high, low = halves(rows_ref[...])
    out_ref[:, below:, :width] = high
    out_ref[:, below:, width:] = low


def places(place_ref, step):
    chans = 8
    mine = place_ref[0]
    twin = mine + 1 - 2 * lax.rem(mine, 2)
    out = []
    for base in (mine, twin):
        for ahead in (0, chans - 2, 2):
            out.append((lax.rem(base + ahead, chans) * step, step))
        far = lax.rem(base + chans // 2, chans) * step
        out.append((far, step // 2))
        out.append((far + step // 2, step // 2))
    return out


def mix_kernel(key_ref, value_ref, out_ref):
    mixed = key_ref[...].astype(jnp.float32) * value_ref[...].astype(jnp.float32)
    out_ref[...] = mixed.reshape(out_ref.shape)


def gate_kernel(place_ref, conv_ref, query_ref, weight_ref, *refs):
    blocks, (both_ref, mid_ref, sem) = refs[:10], refs[10:]
    step = blocks[0].shape[0]
    seqs, rows, width = conv_ref.shape
    copy = pltpu.make_async_copy(conv_ref, both_ref.at[:, :, :width], sem)
    copy.start()
    total = None
    for (start, size), block in zip(places(place_ref, step), blocks):
        columns = weight_ref[:, pl.ds(pl.multiple_of(start, WIDE), size)]
        term = dot(columns, block[...])
        total = term if total is None else total + term
    mid_ref[...] = total
    gate = query_ref[...].astype(jnp.float32) * total
    both_ref[:, :, width:] = gate.astype(jnp.bfloat16).reshape(seqs, rows, width // 2)
    copy.wait()


def part_kernel(place_ref, both_ref, query_ref, *refs):
    blocks, (part_ref,) = refs[:10], refs[10:]
    step = blocks[0].shape[0]
    channels, width = query_ref.shape
    both = both_ref[:, :, : 2 * width].astype(jnp.float32)
    conv_out = (both[:, :, :width] + both[:, :, width:]).reshape(channels, width)
    gated = (query_ref[...].astype(jnp.float32) * conv_out).astype(jnp.bfloat16)
    for (start, size), block in zip(places(place_ref, step), blocks):
        term = lax.dot_general(
            gated, block[...], (((1,), (1,)), ((), ())), preferred_element_type=jnp.float32
        )
        part_ref[:, pl.ds(pl.multiple_of(start, WIDE), size)] = term.astype(jnp.bfloat16)


def total_kernel(scale, part_ref, out_ref):
    group, rows, features = part_ref.shape
    half = features // 2
    total = part_ref[0].astype(jnp.float32)
    for source in range(1, group):
        total = total + part_ref[source].astype(jnp.float32)
    total = (total * scale).astype(jnp.bfloat16)
    out_ref[:rows, :] = total[:, :half]
    out_ref[rows:, :] = total[:, half:]


def last_kernel(mine_ref, other_ref, back_ref, out_ref, sems):
    rows = mine_ref.shape[0]
    copies = []
    for target in range(out_ref.shape[0]):
        for turn, source in enumerate((mine_ref, other_ref)):
            place = out_ref.at[target, turn * rows : (turn + 1) * rows, :]
            copies.append(pltpu.make_async_copy(source, place, sems.at[target, turn]))
    for copy in copies:
        copy.start()
    for copy in copies:
        copy.wait()


def final_kernel(dp_ref, all_ref, key_ref, value_ref, grad_key_ref, grad_value_ref, grad_weight_ref):
    seqs, _, half = all_ref.shape
    channels, span = key_ref.shape
    rows = channels // (2 * seqs)
    lanes = channels // seqs
    for source in range(seqs):
        for turn in range(2):
            owner = dp_ref[0] + turn - 2 * turn * dp_ref[0]
            place = pl.ds(pl.multiple_of(owner * (channels // 2) + source * rows, 8), rows)
            piece = all_ref[source, 2 * turn * rows : 2 * (turn + 1) * rows, :].astype(jnp.float32)
            grad_weight_ref[place, :half] = piece[:rows]
            grad_weight_ref[place, half:] = piece[rows:]
        both = all_ref[source, 4 * rows :, :].astype(jnp.float32)
        mixed = both[:, :span] + both[:, span:]
        place = slice(source * lanes, (source + 1) * lanes)
        grad_key_ref[place, :] = (mixed * value_ref[place, :].astype(jnp.float32)).astype(jnp.bfloat16)
        grad_value_ref[place, :] = (mixed * key_ref[place, :].astype(jnp.float32)).astype(jnp.bfloat16)


def fixed(values):
    return pltpu.with_memory_space_constraint(values, pltpu.HBM)


def limited(mebibytes):
    return pltpu.CompilerParams(vmem_limit_bytes=mebibytes * 1024 * 1024)


def convolve(signal, filt, natural, tables):
    blocks, channels, width = signal.shape
    return pl.pallas_call(
        convolve_kernel,
        out_shape=(
            jax.ShapeDtypeStruct((blocks, channels, 2 * width), jnp.bfloat16),
            jax.ShapeDtypeStruct((channels // BATCH, BATCH * TALL, 2 * WIDE), jnp.float32),
        ),
        scratch_shapes=[
            pltpu.VMEM((TALL, channels, WIDE), jnp.float32),
            pltpu.VMEM(signal.shape, jnp.float32),
        ],
        name="convolve",
        compiler_params=limited(40),
        cost_estimate=pl.CostEstimate(flops=4_000_000_000, bytes_accessed=3_000_000, transcendentals=0),
    )(signal, filt, natural, *tables)


def correlate(both, spec, tables, above):
    blocks, channels, triple = both.shape
    width = triple // 3
    return pl.pallas_call(
        correlate_kernel,
        out_shape=jax.ShapeDtypeStruct((blocks, above + channels, 2 * width), jnp.bfloat16),
        scratch_shapes=[pltpu.VMEM((blocks, channels, width), jnp.float32)] * 2,
        name="correlate",
        cost_estimate=pl.CostEstimate(flops=4_000_000_000, bytes_accessed=3_000_000, transcendentals=0),
    )(both, spec, *tables)


def placed_call(kernel, count, out_shape, left=()):
    whole = pl.BlockSpec(memory_space=pltpu.VMEM)
    return pl.pallas_call(
        kernel,
        in_specs=[pl.BlockSpec(memory_space=pltpu.SMEM)]
        + [pl.BlockSpec(memory_space=pltpu.HBM)] * len(left)
        + [whole] * (count - len(left)),
        scratch_shapes=[pltpu.SemaphoreType.DMA] * len(left),
        out_shape=out_shape,
        compiler_params=limited(LIMIT),
        cost_estimate=pl.CostEstimate(flops=600_000_000, bytes_accessed=5_000_000, transcendentals=0),
    )


def gather_features(block, chans):
    def send(values, hop):
        return lax.ppermute(values, "chan", [(k, hop(k)) for k in range(chans)])

    def ahead(k):
        return (k + 2) % chans

    def behind(k):
        return (k - 2) % chans

    half = block.shape[0] // 2
    from_behind = send(block, ahead)
    from_ahead = send(block, behind)
    far_top = send(from_behind[:half], ahead)
    far_bottom = send(from_ahead[half:], behind)
    mine = [block, from_behind, from_ahead, far_top, far_bottom]
    return mine + [send(values, lambda k: k ^ 1) for values in mine]


def swap(blocks, axes="seq"):
    return lax.all_to_all(blocks, axes, split_axis=0, concat_axis=0, tiled=True)


def shards(query_proj, key_proj, value_proj, grad_out, out_weight, long_filter):
    rows, length = long_filter.shape
    seqs, chans, dps = lax.axis_size("seq"), lax.axis_size("chan"), lax.axis_size("dp")
    channels, span = query_proj.shape[1:]
    features = out_weight.shape[1]
    pieces = span // WIDE
    arrived = (np.arange(seqs)[None, :] * pieces + np.arange(pieces)[:, None]).reshape(-1)
    twist, there, back = make_shared()
    analyse_natural, _ = make_tables(np.arange(TALL))
    analyse, restore = make_tables(arrived)
    tables = tuple(fixed(jnp.asarray(t)) for t in (analyse, restore, twist, there, back))
    place = lax.axis_index("chan").astype(jnp.int32).reshape(1)

    blocks = gather_features(grad_out[0], chans)
    mixed_in = pl.pallas_call(
        mix_kernel,
        out_shape=jax.ShapeDtypeStruct((seqs, rows, span), jnp.float32),
        name="mix",
    )(key_proj[0], value_proj[0])
    mixed_full = swap(mixed_in)
    conv_full, spec = convolve(mixed_full, fixed(long_filter), fixed(jnp.asarray(analyse_natural)), tables)

    both, grad_mid = placed_call(
        gate_kernel,
        13,
        (
            jax.ShapeDtypeStruct((seqs, rows, 3 * span), jnp.bfloat16),
            jax.ShapeDtypeStruct((channels, span), jnp.float32),
        ),
        left=(0,),
    )(place, fixed(conv_full), query_proj[0], out_weight, *blocks)
    both = swap(both)
    weight_part = placed_call(
        part_kernel, 12, jax.ShapeDtypeStruct((channels, features), jnp.bfloat16)
    )(place, both, query_proj[0], *blocks)
    conv_out = both[:, :, :span].astype(jnp.float32) + both[:, :, span : 2 * span].astype(jnp.float32)
    grad_query = (grad_mid * conv_out.reshape(channels, span)).astype(jnp.bfloat16)

    group = dps * seqs
    weight_part = swap(weight_part.reshape(group, channels // group, features), ("dp", "seq"))
    back_full = correlate(both, spec, tables, 4 * (channels // group))
    scale = 1.0 / math.sqrt(dps * length)
    half = features // 2
    mine = pl.pallas_call(
        lambda *refs: total_kernel(scale, *refs),
        out_shape=jax.ShapeDtypeStruct((2 * (channels // group), half), jnp.bfloat16),
        name="total",
        compiler_params=limited(LIMIT),
    )(weight_part)
    other = lax.ppermute(mine, "dp", [(0, 1), (1, 0)])
    whole = pl.BlockSpec(memory_space=pltpu.VMEM)
    left = pl.BlockSpec(memory_space=pltpu.HBM)
    last = pl.pallas_call(
        last_kernel,
        in_specs=[whole, whole, left],
        out_specs=left,
        out_shape=jax.ShapeDtypeStruct(back_full.shape, back_full.dtype),
        input_output_aliases={2: 0},
        scratch_shapes=[pltpu.SemaphoreType.DMA((seqs, 2))],
        name="last",
        compiler_params=limited(LIMIT),
    )(mine, other, fixed(back_full))
    last = swap(last)
    grad_key, grad_value, grad_weight = placed_call(
        final_kernel,
        3,
        (
            jax.ShapeDtypeStruct((channels, span), jnp.bfloat16),
            jax.ShapeDtypeStruct((channels, span), jnp.bfloat16),
            jax.ShapeDtypeStruct((channels, features), jnp.float32),
        ),
    )(lax.axis_index("dp").astype(jnp.int32).reshape(1), last, key_proj[0], value_proj[0])
    return (grad_query[None], grad_key[None], grad_value[None], grad_weight)


def solution(mesh):
    placed = (
        P("dp", "chan", "seq"),
        P("dp", "chan", "seq"),
        P("dp", "chan", "seq"),
        P("dp", "chan", "seq"),
        P("chan", None),
        P(("chan", "seq"), None),
    )
    return jax.shard_map(
        shards,
        mesh=mesh,
        in_specs=placed,
        out_specs=(
            P("dp", "chan", "seq"),
            P("dp", "chan", "seq"),
            P("dp", "chan", "seq"),
            P("chan", None),
        ),
        check_vma=False,
    )
```

```python
import math

import jax
import jax.numpy as jnp
import ml_dtypes
import numpy as np
from jax import lax
from jax.experimental import pallas as pl
from jax.experimental.pallas import tpu as pltpu
from jax.sharding import PartitionSpec as P


WIDE = 128
TALL = 64
LIMIT = 20
BATCH = 16


def split_table(values):
    high = values.astype(ml_dtypes.bfloat16)
    low = (values - high.astype(np.float64)).astype(ml_dtypes.bfloat16)
    return high, low


def make_tables(row_of):
    freq = np.arange(TALL) + 0.25
    first = 2.0 * np.pi / TALL * freq[:, None] * np.asarray(row_of)[None, :]
    first = np.concatenate([np.cos(first), -np.sin(first)], axis=0)
    high, low = split_table(first)
    analyse = np.concatenate([high, high, low], axis=1)
    last = 2.0 * np.pi / TALL * np.asarray(row_of)[:, None] * freq[None, :]
    last = np.concatenate([np.cos(last), -np.sin(last)], axis=1) / (TALL * WIDE)
    high, low = split_table(last)
    restore = np.concatenate([high, high, low], axis=1)
    return analyse, restore


def make_shared():
    freq = np.arange(TALL) + 0.25
    cols = np.arange(WIDE)
    turn = 2.0 * np.pi / (TALL * WIDE) * freq[:, None] * cols[None, :]
    twist = np.stack([np.cos(turn), np.sin(turn)]).astype(np.float32)
    angle = 2.0 * np.pi / WIDE * (cols[:, None] * cols[None, :] % WIDE)
    cos, sin = np.cos(angle), np.sin(angle)
    there = np.concatenate([np.concatenate([cos, -sin], 1), np.concatenate([sin, cos], 1)], 0)
    back = np.concatenate([np.concatenate([cos, sin], 1), np.concatenate([-sin, cos], 1)], 0)
    out = []
    for table in (there, back):
        high, low = split_table(table)
        out.append(np.concatenate([high, high, low], axis=0))
    return twist, out[0], out[1]


def halves(values):
    high = values.astype(jnp.bfloat16)
    low = (values - high.astype(jnp.float32)).astype(jnp.bfloat16)
    return high, low


def dot(left, right):
    return jnp.dot(left, right, preferred_element_type=jnp.float32)


def stacked(values):
    high, low = halves(values)
    return jnp.concatenate([high, low, high], axis=0)


def beside(values):
    high, low = halves(values)
    return jnp.concatenate([high, low, high], axis=1)


def forward_group(inputs, analyse, twist, there):
    both = dot(analyse, stacked(jnp.concatenate(inputs, axis=1)))
    cos, sin = twist[0], twist[1]
    rows = []
    for which in range(len(inputs)):
        real = both[:TALL, which * WIDE : (which + 1) * WIDE]
        imag = both[TALL:, which * WIDE : (which + 1) * WIDE]
        rows.append(jnp.concatenate([real * cos + imag * sin, imag * cos - real * sin], axis=1))
    return dot(beside(jnp.concatenate(rows, axis=0)), there)


def inverse_group(spec, restore, twist, back):
    both = dot(beside(spec), back)
    cos, sin = twist[0], twist[1]
    columns = []
    for which in range(spec.shape[0] // TALL):
        real = both[which * TALL : (which + 1) * TALL, :WIDE]
        imag = both[which * TALL : (which + 1) * TALL, WIDE:]
        columns.append(jnp.concatenate([real * cos - imag * sin, real * sin + imag * cos], axis=0))
    return dot(restore, stacked(jnp.concatenate(columns, axis=1)))


def product(left, right, conjugate):
    real, imag = left[:, :WIDE], left[:, WIDE:]
    other_real, other_imag = right[:, :WIDE], right[:, WIDE:]
    if conjugate:
        other_imag = -other_imag
    return jnp.concatenate(
        [real * other_real - imag * other_imag, real * other_imag + imag * other_real], axis=1
    )


def arrived_rows(signal_ref, channel, offset, width):
    rows = signal_ref[:, channel, offset : offset + width]
    return jnp.concatenate([rows[:, q * WIDE : (q + 1) * WIDE] for q in range(width // WIDE)], axis=0)


def sent_rows(result, which, blocks):
    column = result[:, which * WIDE : (which + 1) * WIDE]
    return jnp.concatenate(
        [column[q * blocks : (q + 1) * blocks] for q in range(TALL // blocks)], axis=1
    )


def convolve_kernel(signal_ref, filt_ref, natural_ref, analyse_ref, restore_ref, twist_ref, there_ref, back_ref, out_ref, spec_ref, rows_ref):
    twist = twist_ref[...]
    blocks, channels, width = out_ref.shape
    for place in range(TALL):
        rows_ref[place] = filt_ref[:, place * WIDE : (place + 1) * WIDE]
    for group in range(channels // BATCH):
        members = range(group * BATCH, (group + 1) * BATCH)
        filt = forward_group([rows_ref[:, m, :] for m in members], natural_ref[...], twist, there_ref[...])
        spec_ref[group] = filt
        inputs = [arrived_rows(signal_ref, m, 0, width) for m in members]
        spec = forward_group(inputs, analyse_ref[...], twist, there_ref[...])
        result = inverse_group(product(spec, filt, False), restore_ref[...], twist, back_ref[...])
        for which, m in enumerate(members):
            out_ref[:, m, :] = sent_rows(result, which, blocks)


def correlate_kernel(arrived_ref, spec_ref, analyse_ref, restore_ref, twist_ref, there_ref, back_ref, out_ref, signal_ref, rows_ref):
    twist = twist_ref[...]
    blocks, channels, width = rows_ref.shape
    below = out_ref.shape[1] - channels
    both = arrived_ref[:, below:, :].astype(jnp.float32)
    signal_ref[:, : channels // 2, :] = both[:, :, :width]
    signal_ref[:, channels // 2 :, :] = both[:, :, width:]
    for group in range(channels // BATCH):
        members = range(group * BATCH, (group + 1) * BATCH)
        inputs = [arrived_rows(signal_ref, m, 0, width) for m in members]
        spec = forward_group(inputs, analyse_ref[...], twist, there_ref[...])
        result = inverse_group(product(spec, spec_ref[group], True), restore_ref[...], twist, back_ref[...])
        for which, m in enumerate(members):
            rows_ref[:, m, :] = sent_rows(result, which, blocks)
    high, low = halves(rows_ref[...])
    out_ref[:, below:, :width] = high
    out_ref[:, below:, width:] = low


def places(place_ref, step):
    chans = 8
    mine = place_ref[0]
    twin = mine + 1 - 2 * lax.rem(mine, 2)
    out = []
    for base in (mine, twin):
        for ahead in (0, chans - 2, 2):
            out.append((lax.rem(base + ahead, chans) * step, step))
        far = lax.rem(base + chans // 2, chans) * step
        out.append((far, step // 2))
        out.append((far + step // 2, step // 2))
    return out


def mix_kernel(key_ref, value_ref, out_ref):
    mixed = key_ref[...].astype(jnp.float32) * value_ref[...].astype(jnp.float32)
    out_ref[...] = mixed.reshape(out_ref.shape)


def middle_kernel(place_ref, conv_ref, query_ref, weight_ref, *refs):
    blocks, (send_ref, grad_ref) = refs[:10], refs[10:]
    step = blocks[0].shape[0]
    channels, width = query_ref.shape
    seqs, _, half = send_ref.shape
    rows = channels // seqs
    query = query_ref[...].astype(jnp.float32)
    conv_out = conv_ref[...]
    gated = (query * conv_out).astype(jnp.bfloat16)
    total = None
    for (start, size), block in zip(places(place_ref, step), blocks):
        columns = weight_ref[:, pl.ds(pl.multiple_of(start, WIDE), size)]
        term = dot(columns, block[...])
        total = term if total is None else total + term
        part = lax.dot_general(
            gated, block[...], (((1,), (1,)), ((), ())), preferred_element_type=jnp.float32
        )
        upper = pl.multiple_of(start // half * rows, rows)
        lane = pl.multiple_of(lax.rem(start, half), WIDE)
        send_ref[:, pl.ds(upper, rows), pl.ds(lane, size)] = part.astype(jnp.bfloat16).reshape(
            seqs, rows, size
        )
    grad_ref[...] = (total * conv_out).astype(jnp.bfloat16)
    gate = (query * total).astype(jnp.bfloat16).reshape(seqs, rows, width)
    send_ref[:, 2 * rows :, :width] = gate[:, : rows // 2]
    send_ref[:, 2 * rows :, width:] = gate[:, rows // 2 :]


def total_kernel(arrived_ref, out_ref):
    rows = out_ref.shape[0]
    total = arrived_ref[0, :rows, :].astype(jnp.float32)
    for source in range(1, arrived_ref.shape[0]):
        total = total + arrived_ref[source, :rows, :].astype(jnp.float32)
    out_ref[...] = total


def last_kernel(scale, mine_ref, other_ref, back_ref, out_ref, sums_ref, sems):
    rows = mine_ref.shape[0]
    sums_ref[...] = ((mine_ref[...] + other_ref[...]) * scale).astype(jnp.bfloat16)
    copies = [
        pltpu.make_async_copy(sums_ref, out_ref.at[target, :rows, :], sems.at[target])
        for target in range(out_ref.shape[0])
    ]
    for copy in copies:
        copy.start()
    for copy in copies:
        copy.wait()


def final_kernel(all_ref, key_ref, value_ref, grad_key_ref, grad_value_ref, grad_weight_ref):
    seqs, _, half = all_ref.shape
    channels, span = key_ref.shape
    rows = channels // seqs
    for source in range(seqs):
        piece = all_ref[source].astype(jnp.float32)
        place = slice(source * rows, (source + 1) * rows)
        grad_weight_ref[place, :half] = piece[:rows]
        grad_weight_ref[place, half:] = piece[rows : 2 * rows]
        mixed = piece[2 * rows :, :span] + piece[2 * rows :, span:]
        grad_key_ref[place, :] = (mixed * value_ref[place, :].astype(jnp.float32)).astype(jnp.bfloat16)
        grad_value_ref[place, :] = (mixed * key_ref[place, :].astype(jnp.float32)).astype(jnp.bfloat16)


def limited(mebibytes):
    return pltpu.CompilerParams(vmem_limit_bytes=mebibytes * 1024 * 1024)


def convolve(signal, filt, natural, tables):
    _, channels, _ = signal.shape
    return pl.pallas_call(
        convolve_kernel,
        out_shape=(
            jax.ShapeDtypeStruct(signal.shape, jnp.float32),
            jax.ShapeDtypeStruct((channels // BATCH, BATCH * TALL, 2 * WIDE), jnp.float32),
        ),
        scratch_shapes=[pltpu.VMEM((TALL, channels, WIDE), jnp.float32)],
        name="convolve",
        cost_estimate=pl.CostEstimate(flops=4_000_000_000, bytes_accessed=3_000_000, transcendentals=0),
    )(signal, filt, natural, *tables)


def correlate(arrived, spec, tables):
    blocks, depth, double = arrived.shape
    channels = depth * 2 // 5
    shape = (blocks, channels, double // 2)
    return pl.pallas_call(
        correlate_kernel,
        out_shape=jax.ShapeDtypeStruct((blocks, 3 * channels, double), jnp.bfloat16),
        scratch_shapes=[pltpu.VMEM(shape, jnp.float32)] * 2,
        name="correlate",
        cost_estimate=pl.CostEstimate(flops=4_000_000_000, bytes_accessed=3_000_000, transcendentals=0),
    )(arrived, spec, *tables)


def gather_features(block, chans):
    def send(values, hop):
        return lax.ppermute(values, "chan", [(k, hop(k)) for k in range(chans)])

    def ahead(k):
        return (k + 2) % chans

    def behind(k):
        return (k - 2) % chans

    half = block.shape[0] // 2
    from_behind = send(block, ahead)
    from_ahead = send(block, behind)
    far_top = send(from_behind[:half], ahead)
    far_bottom = send(from_ahead[half:], behind)
    mine = [block, from_behind, from_ahead, far_top, far_bottom]
    return mine + [send(values, lambda k: k ^ 1) for values in mine]


def swap(blocks, axes="seq"):
    return lax.all_to_all(blocks, axes, split_axis=0, concat_axis=0, tiled=True)


def shards(query_proj, key_proj, value_proj, grad_out, out_weight, long_filter):
    rows, length = long_filter.shape
    seqs, chans, dps = lax.axis_size("seq"), lax.axis_size("chan"), lax.axis_size("dp")
    channels, span = query_proj.shape[1:]
    features = out_weight.shape[1]
    pieces = span // WIDE
    arrived = (np.arange(seqs)[None, :] * pieces + np.arange(pieces)[:, None]).reshape(-1)
    twist, there, back = make_shared()
    analyse_natural, _ = make_tables(np.arange(TALL))
    analyse, restore = make_tables(arrived)
    tables = tuple(jnp.asarray(t) for t in (analyse, restore, twist, there, back))
    place = lax.axis_index("chan").astype(jnp.int32).reshape(1)

    blocks = gather_features(grad_out[0], chans)
    mixed_in = pl.pallas_call(
        mix_kernel,
        out_shape=jax.ShapeDtypeStruct((seqs, rows, span), jnp.float32),
        name="mix",
    )(key_proj[0], value_proj[0])
    mixed_full = swap(mixed_in)
    conv_full, spec = convolve(mixed_full, long_filter, jnp.asarray(analyse_natural), tables)

    conv_out = swap(conv_full).reshape(channels, span)
    whole = pl.BlockSpec(memory_space=pltpu.VMEM)
    shape = (seqs, 3 * rows, 2 * span)
    send, grad_query = pl.pallas_call(
        middle_kernel,
        in_specs=[pl.BlockSpec(memory_space=pltpu.SMEM)] + [whole] * 13,
        out_shape=(
            jax.ShapeDtypeStruct((seqs, 2 * rows + rows // 2, 2 * span), jnp.bfloat16),
            jax.ShapeDtypeStruct((channels, span), jnp.bfloat16),
        ),
        name="middle",
        compiler_params=limited(LIMIT),
        cost_estimate=pl.CostEstimate(flops=1_200_000_000, bytes_accessed=5_000_000, transcendentals=0),
    )(place, conv_out, query_proj[0], out_weight, *blocks)
    arrived = swap(send)

    mine = pl.pallas_call(
        total_kernel,
        out_shape=jax.ShapeDtypeStruct((2 * rows, 2 * span), jnp.float32),
        name="total",
        compiler_params=limited(LIMIT),
    )(arrived)
    other = lax.ppermute(mine, "dp", [(0, 1), (1, 0)])
    back_full = correlate(arrived, spec, tables)
    scale = 1.0 / math.sqrt(dps * length)
    left = pl.BlockSpec(memory_space=pltpu.HBM)
    last = pl.pallas_call(
        lambda *refs: last_kernel(scale, *refs),
        in_specs=[whole, whole, left],
        out_specs=left,
        out_shape=jax.ShapeDtypeStruct(shape, jnp.bfloat16),
        input_output_aliases={2: 0},
        scratch_shapes=[pltpu.VMEM((2 * rows, 2 * span), jnp.bfloat16), pltpu.SemaphoreType.DMA((seqs,))],
        name="last",
        compiler_params=limited(LIMIT),
    )(mine, other, pltpu.with_memory_space_constraint(back_full, pltpu.HBM))
    last = swap(last)
    grad_key, grad_value, grad_weight = pl.pallas_call(
        final_kernel,
        out_shape=(
            jax.ShapeDtypeStruct((channels, span), jnp.bfloat16),
            jax.ShapeDtypeStruct((channels, span), jnp.bfloat16),
            jax.ShapeDtypeStruct((channels, features), jnp.float32),
        ),
        name="final",
        compiler_params=limited(LIMIT),
    )(last, key_proj[0], value_proj[0])
    return (grad_query[None], grad_key[None], grad_value[None], grad_weight)


def solution(mesh):
    placed = (
        P("dp", "chan", "seq"),
        P("dp", "chan", "seq"),
        P("dp", "chan", "seq"),
        P("dp", "chan", "seq"),
        P("chan", None),
        P(("chan", "seq"), None),
    )
    return jax.shard_map(
        shards,
        mesh=mesh,
        in_specs=placed,
        out_specs=(
            P("dp", "chan", "seq"),
            P("dp", "chan", "seq"),
            P("dp", "chan", "seq"),
            P("chan", None),
        ),
        check_vma=False,
    )
```

```python
import math

import jax
import jax.numpy as jnp
import ml_dtypes
import numpy as np
from jax import lax
from jax.experimental import pallas as pl
from jax.experimental.pallas import tpu as pltpu
from jax.sharding import PartitionSpec as P


WIDE = 128
TALL = 64
LIMIT = 20
BATCH = 16


def split_table(values):
    high = values.astype(ml_dtypes.bfloat16)
    low = (values - high.astype(np.float64)).astype(ml_dtypes.bfloat16)
    return high, low


def make_tables(row_of):
    freq = np.arange(TALL) + 0.25
    first = 2.0 * np.pi / TALL * freq[:, None] * np.asarray(row_of)[None, :]
    first = np.concatenate([np.cos(first), -np.sin(first)], axis=0)
    high, low = split_table(first)
    analyse = np.concatenate([high, high, low], axis=1)
    last = 2.0 * np.pi / TALL * np.asarray(row_of)[:, None] * freq[None, :]
    last = np.concatenate([np.cos(last), -np.sin(last)], axis=1) / (TALL * WIDE)
    high, low = split_table(last)
    restore = np.concatenate([high, high, low], axis=1)
    return analyse, restore


def make_shared():
    freq = np.arange(TALL) + 0.25
    cols = np.arange(WIDE)
    turn = 2.0 * np.pi / (TALL * WIDE) * freq[:, None] * cols[None, :]
    twist = np.stack([np.cos(turn), np.sin(turn)]).astype(np.float32)
    angle = 2.0 * np.pi / WIDE * (cols[:, None] * cols[None, :] % WIDE)
    cos, sin = np.cos(angle), np.sin(angle)
    there = np.concatenate([np.concatenate([cos, -sin], 1), np.concatenate([sin, cos], 1)], 0)
    back = np.concatenate([np.concatenate([cos, sin], 1), np.concatenate([-sin, cos], 1)], 0)
    out = []
    for table in (there, back):
        high, low = split_table(table)
        out.append(np.concatenate([high, high, low], axis=0))
    return twist, out[0], out[1]


def halves(values):
    high = values.astype(jnp.bfloat16)
    low = (values - high.astype(jnp.float32)).astype(jnp.bfloat16)
    return high, low


def dot(left, right):
    return jnp.dot(left, right, preferred_element_type=jnp.float32)


def stacked(values):
    high, low = halves(values)
    return jnp.concatenate([high, low, high], axis=0)


def beside(values):
    high, low = halves(values)
    return jnp.concatenate([high, low, high], axis=1)


def forward_group(inputs, analyse, twist, there):
    both = dot(analyse, stacked(jnp.concatenate(inputs, axis=1)))
    cos, sin = twist[0], twist[1]
    rows = []
    for which in range(len(inputs)):
        real = both[:TALL, which * WIDE : (which + 1) * WIDE]
        imag = both[TALL:, which * WIDE : (which + 1) * WIDE]
        rows.append(jnp.concatenate([real * cos + imag * sin, imag * cos - real * sin], axis=1))
    return dot(beside(jnp.concatenate(rows, axis=0)), there)


def inverse_group(spec, restore, twist, back):
    both = dot(beside(spec), back)
    cos, sin = twist[0], twist[1]
    columns = []
    for which in range(spec.shape[0] // TALL):
        real = both[which * TALL : (which + 1) * TALL, :WIDE]
        imag = both[which * TALL : (which + 1) * TALL, WIDE:]
        columns.append(jnp.concatenate([real * cos - imag * sin, real * sin + imag * cos], axis=0))
    return dot(restore, stacked(jnp.concatenate(columns, axis=1)))


def product(left, right, conjugate):
    real, imag = left[:, :WIDE], left[:, WIDE:]
    other_real, other_imag = right[:, :WIDE], right[:, WIDE:]
    if conjugate:
        other_imag = -other_imag
    return jnp.concatenate(
        [real * other_real - imag * other_imag, real * other_imag + imag * other_real], axis=1
    )


def arrived_rows(signal_ref, channel, offset, width):
    rows = signal_ref[:, channel, offset : offset + width]
    return jnp.concatenate([rows[:, q * WIDE : (q + 1) * WIDE] for q in range(width // WIDE)], axis=0)


def sent_rows(result, which, blocks):
    column = result[:, which * WIDE : (which + 1) * WIDE]
    return jnp.concatenate(
        [column[q * blocks : (q + 1) * blocks] for q in range(TALL // blocks)], axis=1
    )


def convolve_kernel(signal_ref, filt_ref, natural_ref, analyse_ref, restore_ref, twist_ref, there_ref, back_ref, out_ref, spec_ref, rows_ref):
    twist = twist_ref[...]
    blocks, channels, width = out_ref.shape
    for place in range(TALL):
        rows_ref[place] = filt_ref[:, place * WIDE : (place + 1) * WIDE]
    for group in range(channels // BATCH):
        members = range(group * BATCH, (group + 1) * BATCH)
        filt = forward_group([rows_ref[:, m, :] for m in members], natural_ref[...], twist, there_ref[...])
        spec_ref[group] = filt
        inputs = [arrived_rows(signal_ref, m, 0, width) for m in members]
        spec = forward_group(inputs, analyse_ref[...], twist, there_ref[...])
        result = inverse_group(product(spec, filt, False), restore_ref[...], twist, back_ref[...])
        for which, m in enumerate(members):
            out_ref[:, m, :] = sent_rows(result, which, blocks)


def correlate_kernel(arrived_ref, spec_ref, analyse_ref, restore_ref, twist_ref, there_ref, back_ref, out_ref, signal_ref, rows_ref):
    twist = twist_ref[...]
    blocks, channels, width = rows_ref.shape
    below = arrived_ref.shape[1] - channels // 2
    both = arrived_ref[:, below:, :].astype(jnp.float32)
    signal_ref[:, : channels // 2, :] = both[:, :, :width]
    signal_ref[:, channels // 2 :, :] = both[:, :, width:]
    for group in range(channels // BATCH):
        members = range(group * BATCH, (group + 1) * BATCH)
        inputs = [arrived_rows(signal_ref, m, 0, width) for m in members]
        spec = forward_group(inputs, analyse_ref[...], twist, there_ref[...])
        result = inverse_group(product(spec, spec_ref[group], True), restore_ref[...], twist, back_ref[...])
        for which, m in enumerate(members):
            rows_ref[:, m, :] = sent_rows(result, which, blocks)
    high, low = halves(rows_ref[...])
    out_ref[:, :, :width] = high
    out_ref[:, :, width:] = low


def places(place_ref, step):
    chans = 8
    mine = place_ref[0]
    twin = mine + 1 - 2 * lax.rem(mine, 2)
    out = []
    for base in (mine, twin):
        for ahead in (0, chans - 2, 2):
            out.append((lax.rem(base + ahead, chans) * step, step))
        far = lax.rem(base + chans // 2, chans) * step
        out.append((far, step // 2))
        out.append((far + step // 2, step // 2))
    return out


def mix_kernel(key_ref, value_ref, out_ref):
    mixed = key_ref[...].astype(jnp.float32) * value_ref[...].astype(jnp.float32)
    out_ref[...] = mixed.reshape(out_ref.shape)


def middle_kernel(place_ref, conv_ref, query_ref, weight_ref, *refs):
    blocks, (send_ref, grad_ref) = refs[:10], refs[10:]
    step = blocks[0].shape[0]
    channels, width = query_ref.shape
    seqs, _, half = send_ref.shape
    rows = channels // seqs
    query = query_ref[...].astype(jnp.float32)
    conv_out = conv_ref[...]
    gated = (query * conv_out).astype(jnp.bfloat16)
    total = None
    for (start, size), block in zip(places(place_ref, step), blocks):
        columns = weight_ref[:, pl.ds(pl.multiple_of(start, WIDE), size)]
        term = dot(columns, block[...])
        total = term if total is None else total + term
        part = lax.dot_general(
            gated, block[...], (((1,), (1,)), ((), ())), preferred_element_type=jnp.float32
        )
        upper = pl.multiple_of(start // half * rows, rows)
        lane = pl.multiple_of(lax.rem(start, half), WIDE)
        send_ref[:, pl.ds(upper, rows), pl.ds(lane, size)] = part.astype(jnp.bfloat16).reshape(
            seqs, rows, size
        )
    grad_ref[...] = (total * conv_out).astype(jnp.bfloat16)
    gate = (query * total).astype(jnp.bfloat16).reshape(seqs, rows, width)
    send_ref[:, 2 * rows :, :width] = gate[:, : rows // 2]
    send_ref[:, 2 * rows :, width:] = gate[:, rows // 2 :]


def total_kernel(arrived_ref, out_ref):
    rows = out_ref.shape[0]
    total = arrived_ref[0, :rows, :].astype(jnp.float32)
    for source in range(1, arrived_ref.shape[0]):
        total = total + arrived_ref[source, :rows, :].astype(jnp.float32)
    out_ref[...] = total


def last_kernel(scale, mine_ref, other_ref, back_ref, out_ref):
    rows, half = mine_ref.shape
    sums = ((mine_ref[...] + other_ref[...]) * scale).astype(jnp.bfloat16)
    out_ref[:, :rows, :] = jnp.broadcast_to(sums[None], (out_ref.shape[0], rows, half))
    out_ref[:, rows:, :] = back_ref[...]


def final_kernel(all_ref, key_ref, value_ref, grad_key_ref, grad_value_ref, grad_weight_ref):
    seqs, _, half = all_ref.shape
    channels, span = key_ref.shape
    rows = channels // seqs
    for source in range(seqs):
        piece = all_ref[source].astype(jnp.float32)
        place = slice(source * rows, (source + 1) * rows)
        grad_weight_ref[place, :half] = piece[:rows]
        grad_weight_ref[place, half:] = piece[rows : 2 * rows]
        mixed = piece[2 * rows :, :span] + piece[2 * rows :, span:]
        grad_key_ref[place, :] = (mixed * value_ref[place, :].astype(jnp.float32)).astype(jnp.bfloat16)
        grad_value_ref[place, :] = (mixed * key_ref[place, :].astype(jnp.float32)).astype(jnp.bfloat16)


def fixed(values):
    return pltpu.with_memory_space_constraint(values, pltpu.HBM)


def limited(mebibytes):
    return pltpu.CompilerParams(vmem_limit_bytes=mebibytes * 1024 * 1024)


def convolve(signal, filt, natural, tables):
    _, channels, _ = signal.shape
    return pl.pallas_call(
        convolve_kernel,
        out_shape=(
            jax.ShapeDtypeStruct(signal.shape, jnp.float32),
            jax.ShapeDtypeStruct((channels // BATCH, BATCH * TALL, 2 * WIDE), jnp.float32),
        ),
        scratch_shapes=[pltpu.VMEM((TALL, channels, WIDE), jnp.float32)],
        name="convolve",
        cost_estimate=pl.CostEstimate(flops=4_000_000_000, bytes_accessed=3_000_000, transcendentals=0),
    )(signal, filt, natural, *tables)


def correlate(arrived, spec, tables):
    blocks, depth, double = arrived.shape
    channels = depth * 2 // 5
    shape = (blocks, channels, double // 2)
    return pl.pallas_call(
        correlate_kernel,
        out_shape=jax.ShapeDtypeStruct((blocks, channels, double), jnp.bfloat16),
        scratch_shapes=[pltpu.VMEM(shape, jnp.float32)] * 2,
        name="correlate",
        compiler_params=limited(LIMIT),
        cost_estimate=pl.CostEstimate(flops=4_000_000_000, bytes_accessed=3_000_000, transcendentals=0),
    )(arrived, spec, *tables)


def gather_features(block, chans):
    def send(values, hop):
        return lax.ppermute(values, "chan", [(k, hop(k)) for k in range(chans)])

    def ahead(k):
        return (k + 2) % chans

    def behind(k):
        return (k - 2) % chans

    half = block.shape[0] // 2
    from_behind = send(block, ahead)
    from_ahead = send(block, behind)
    far_top = send(from_behind[:half], ahead)
    far_bottom = send(from_ahead[half:], behind)
    mine = [block, from_behind, from_ahead, far_top, far_bottom]
    return mine + [send(values, lambda k: k ^ 1) for values in mine]


def swap(blocks, axes="seq"):
    return lax.all_to_all(blocks, axes, split_axis=0, concat_axis=0, tiled=True)


def shards(query_proj, key_proj, value_proj, grad_out, out_weight, long_filter):
    rows, length = long_filter.shape
    seqs, chans, dps = lax.axis_size("seq"), lax.axis_size("chan"), lax.axis_size("dp")
    channels, span = query_proj.shape[1:]
    features = out_weight.shape[1]
    pieces = span // WIDE
    arrived = (np.arange(seqs)[None, :] * pieces + np.arange(pieces)[:, None]).reshape(-1)
    twist, there, back = make_shared()
    analyse_natural, _ = make_tables(np.arange(TALL))
    analyse, restore = make_tables(arrived)
    tables = tuple(fixed(jnp.asarray(t)) for t in (analyse, restore, twist, there, back))
    place = lax.axis_index("chan").astype(jnp.int32).reshape(1)

    blocks = gather_features(grad_out[0], chans)
    mixed_in = pl.pallas_call(
        mix_kernel,
        out_shape=jax.ShapeDtypeStruct((seqs, rows, span), jnp.float32),
        name="mix",
    )(key_proj[0], value_proj[0])
    mixed_full = swap(mixed_in)
    conv_full, spec = convolve(mixed_full, long_filter, jnp.asarray(analyse_natural), tables)

    conv_out = swap(conv_full).reshape(channels, span)
    whole = pl.BlockSpec(memory_space=pltpu.VMEM)
    shape = (seqs, 3 * rows, 2 * span)
    send, grad_query = pl.pallas_call(
        middle_kernel,
        in_specs=[pl.BlockSpec(memory_space=pltpu.SMEM)] + [whole] * 13,
        out_shape=(
            jax.ShapeDtypeStruct((seqs, 2 * rows + rows // 2, 2 * span), jnp.bfloat16),
            jax.ShapeDtypeStruct((channels, span), jnp.bfloat16),
        ),
        name="middle",
        compiler_params=limited(LIMIT),
        cost_estimate=pl.CostEstimate(flops=1_200_000_000, bytes_accessed=5_000_000, transcendentals=0),
    )(place, conv_out, query_proj[0], out_weight, *blocks)
    arrived = swap(send)

    mine = pl.pallas_call(
        total_kernel,
        out_shape=jax.ShapeDtypeStruct((2 * rows, 2 * span), jnp.float32),
        name="total",
        compiler_params=limited(LIMIT),
    )(arrived)
    other = lax.ppermute(mine, "dp", [(0, 1), (1, 0)])
    back_full = correlate(arrived, spec, tables)
    scale = 1.0 / math.sqrt(dps * length)
    last = pl.pallas_call(
        lambda *refs: last_kernel(scale, *refs),
        in_specs=[whole] * 3,
        out_specs=whole,
        out_shape=jax.ShapeDtypeStruct(shape, jnp.bfloat16),
        name="last",
        compiler_params=limited(LIMIT),
    )(mine, other, back_full)
    last = swap(last)
    grad_key, grad_value, grad_weight = pl.pallas_call(
        final_kernel,
        out_shape=(
            jax.ShapeDtypeStruct((channels, span), jnp.bfloat16),
            jax.ShapeDtypeStruct((channels, span), jnp.bfloat16),
            jax.ShapeDtypeStruct((channels, features), jnp.float32),
        ),
        name="final",
        compiler_params=limited(LIMIT),
    )(last, key_proj[0], value_proj[0])
    return (grad_query[None], grad_key[None], grad_value[None], grad_weight)


def solution(mesh):
    placed = (
        P("dp", "chan", "seq"),
        P("dp", "chan", "seq"),
        P("dp", "chan", "seq"),
        P("dp", "chan", "seq"),
        P("chan", None),
        P(("chan", "seq"), None),
    )
    return jax.shard_map(
        shards,
        mesh=mesh,
        in_specs=placed,
        out_specs=(
            P("dp", "chan", "seq"),
            P("dp", "chan", "seq"),
            P("dp", "chan", "seq"),
            P("chan", None),
        ),
        check_vma=False,
    )
```

```python
import math

import jax
import jax.numpy as jnp
import ml_dtypes
import numpy as np
from jax import lax
from jax.experimental import pallas as pl
from jax.experimental.pallas import tpu as pltpu
from jax.sharding import PartitionSpec as P


WIDE = 128
TALL = 64
LIMIT = 20
BATCH = 16


def split_table(values):
    high = values.astype(ml_dtypes.bfloat16)
    low = (values - high.astype(np.float64)).astype(ml_dtypes.bfloat16)
    return high, low


def make_tables(row_of):
    freq = np.arange(TALL) + 0.25
    first = 2.0 * np.pi / TALL * freq[:, None] * np.asarray(row_of)[None, :]
    first = np.concatenate([np.cos(first), -np.sin(first)], axis=0)
    high, low = split_table(first)
    analyse = np.concatenate([high, high, low], axis=1)
    last = 2.0 * np.pi / TALL * np.asarray(row_of)[:, None] * freq[None, :]
    last = np.concatenate([np.cos(last), -np.sin(last)], axis=1) / (TALL * WIDE)
    high, low = split_table(last)
    restore = np.concatenate([high, high, low], axis=1)
    return analyse, restore


def make_shared():
    freq = np.arange(TALL) + 0.25
    cols = np.arange(WIDE)
    turn = 2.0 * np.pi / (TALL * WIDE) * freq[:, None] * cols[None, :]
    twist = np.stack([np.cos(turn), np.sin(turn)]).astype(np.float32)
    angle = 2.0 * np.pi / WIDE * (cols[:, None] * cols[None, :] % WIDE)
    cos, sin = np.cos(angle), np.sin(angle)
    there = np.concatenate([np.concatenate([cos, -sin], 1), np.concatenate([sin, cos], 1)], 0)
    back = np.concatenate([np.concatenate([cos, sin], 1), np.concatenate([-sin, cos], 1)], 0)
    out = []
    for table in (there, back):
        high, low = split_table(table)
        out.append(np.concatenate([high, high, low], axis=0))
    return twist, out[0], out[1]


def halves(values):
    high = values.astype(jnp.bfloat16)
    low = (values - high.astype(jnp.float32)).astype(jnp.bfloat16)
    return high, low


def dot(left, right):
    return jnp.dot(left, right, preferred_element_type=jnp.float32)


def stacked(values):
    high, low = halves(values)
    return jnp.concatenate([high, low, high], axis=0)


def beside(values):
    high, low = halves(values)
    return jnp.concatenate([high, low, high], axis=1)


def forward_group(inputs, analyse, twist, there, exact=False):
    signal = jnp.concatenate(inputs, axis=1)
    if exact:
        signal = signal.astype(jnp.bfloat16)
        analyse = jnp.concatenate([analyse[:, :TALL], analyse[:, 2 * TALL :]], axis=1)
        both = dot(analyse, jnp.concatenate([signal, signal], axis=0))
    else:
        both = dot(analyse, stacked(signal))
    cos, sin = twist[0], twist[1]
    rows = []
    for which in range(len(inputs)):
        real = both[:TALL, which * WIDE : (which + 1) * WIDE]
        imag = both[TALL:, which * WIDE : (which + 1) * WIDE]
        rows.append(jnp.concatenate([real * cos + imag * sin, imag * cos - real * sin], axis=1))
    return dot(beside(jnp.concatenate(rows, axis=0)), there)


def inverse_group(spec, restore, twist, back):
    both = dot(beside(spec), back)
    cos, sin = twist[0], twist[1]
    columns = []
    for which in range(spec.shape[0] // TALL):
        real = both[which * TALL : (which + 1) * TALL, :WIDE]
        imag = both[which * TALL : (which + 1) * TALL, WIDE:]
        columns.append(jnp.concatenate([real * cos - imag * sin, real * sin + imag * cos], axis=0))
    return dot(restore, stacked(jnp.concatenate(columns, axis=1)))


def product(left, right, conjugate):
    real, imag = left[:, :WIDE], left[:, WIDE:]
    other_real, other_imag = right[:, :WIDE], right[:, WIDE:]
    if conjugate:
        other_imag = -other_imag
    return jnp.concatenate(
        [real * other_real - imag * other_imag, real * other_imag + imag * other_real], axis=1
    )


def arrived_rows(signal_ref, channel, offset, width):
    rows = signal_ref[:, channel, offset : offset + width]
    return jnp.concatenate([rows[:, q * WIDE : (q + 1) * WIDE] for q in range(width // WIDE)], axis=0)


def sent_rows(result, which, blocks):
    column = result[:, which * WIDE : (which + 1) * WIDE]
    return jnp.concatenate(
        [column[q * blocks : (q + 1) * blocks] for q in range(TALL // blocks)], axis=1
    )


def convolve_kernel(signal_ref, filt_ref, natural_ref, analyse_ref, restore_ref, twist_ref, there_ref, back_ref, out_ref, spec_ref, rows_ref):
    twist = twist_ref[...]
    blocks, channels, width = out_ref.shape
    for place in range(TALL):
        rows_ref[place] = filt_ref[:, place * WIDE : (place + 1) * WIDE]
    for group in range(channels // BATCH):
        members = range(group * BATCH, (group + 1) * BATCH)
        filt = forward_group([rows_ref[:, m, :] for m in members], natural_ref[...], twist, there_ref[...])
        spec_ref[group] = filt
        inputs = [arrived_rows(signal_ref, m, 0, width) for m in members]
        spec = forward_group(inputs, analyse_ref[...], twist, there_ref[...])
        result = inverse_group(product(spec, filt, False), restore_ref[...], twist, back_ref[...])
        for which, m in enumerate(members):
            out_ref[:, m, :] = sent_rows(result, which, blocks)


def correlate_kernel(arrived_ref, spec_ref, analyse_ref, restore_ref, twist_ref, there_ref, back_ref, out_ref, signal_ref, rows_ref):
    twist = twist_ref[...]
    blocks, channels, width = rows_ref.shape
    below = arrived_ref.shape[1] - channels // 2
    both = arrived_ref[:, below:, :].astype(jnp.float32)
    signal_ref[:, : channels // 2, :] = both[:, :, :width]
    signal_ref[:, channels // 2 :, :] = both[:, :, width:]
    for group in range(channels // BATCH):
        members = range(group * BATCH, (group + 1) * BATCH)
        inputs = [arrived_rows(signal_ref, m, 0, width) for m in members]
        spec = forward_group(inputs, analyse_ref[...], twist, there_ref[...], True)
        result = inverse_group(product(spec, spec_ref[group], True), restore_ref[...], twist, back_ref[...])
        for which, m in enumerate(members):
            rows_ref[:, m, :] = sent_rows(result, which, blocks)
    high, low = halves(rows_ref[...])
    out_ref[:, :, :width] = high
    out_ref[:, :, width:] = low


def places(place_ref, step):
    chans = 8
    mine = place_ref[0]
    twin = mine + 1 - 2 * lax.rem(mine, 2)
    out = []
    for base in (mine, twin):
        for ahead in (0, chans - 2, 2):
            out.append((lax.rem(base + ahead, chans) * step, step))
        far = lax.rem(base + chans // 2, chans) * step
        out.append((far, step // 2))
        out.append((far + step // 2, step // 2))
    return out


def mix_kernel(key_ref, value_ref, out_ref):
    mixed = key_ref[...].astype(jnp.float32) * value_ref[...].astype(jnp.float32)
    out_ref[...] = mixed.reshape(out_ref.shape)


def middle_kernel(place_ref, conv_ref, query_ref, weight_ref, *refs):
    blocks, (send_ref, grad_ref) = refs[:10], refs[10:]
    step = blocks[0].shape[0]
    channels, width = query_ref.shape
    seqs, _, half = send_ref.shape
    rows = channels // seqs
    query = query_ref[...].astype(jnp.float32)
    conv_out = conv_ref[...]
    gated = (query * conv_out).astype(jnp.bfloat16)
    total = None
    for (start, size), block in zip(places(place_ref, step), blocks):
        columns = weight_ref[:, pl.ds(pl.multiple_of(start, WIDE), size)]
        term = dot(columns, block[...])
        total = term if total is None else total + term
        part = lax.dot_general(
            gated, block[...], (((1,), (1,)), ((), ())), preferred_element_type=jnp.float32
        )
        upper = pl.multiple_of(start // half * rows, rows)
        lane = pl.multiple_of(lax.rem(start, half), WIDE)
        send_ref[:, pl.ds(upper, rows), pl.ds(lane, size)] = part.astype(jnp.bfloat16).reshape(
            seqs, rows, size
        )
    grad_ref[...] = (total * conv_out).astype(jnp.bfloat16)
    gate = (query * total).astype(jnp.bfloat16).reshape(seqs, rows, width)
    send_ref[:, 2 * rows :, :width] = gate[:, : rows // 2]
    send_ref[:, 2 * rows :, width:] = gate[:, rows // 2 :]


def total_kernel(arrived_ref, out_ref):
    rows = out_ref.shape[0]
    total = arrived_ref[0, :rows, :].astype(jnp.float32)
    for source in range(1, arrived_ref.shape[0]):
        total = total + arrived_ref[source, :rows, :].astype(jnp.float32)
    out_ref[...] = total


def last_kernel(scale, mine_ref, other_ref, back_ref, out_ref):
    rows, half = mine_ref.shape
    sums = ((mine_ref[...] + other_ref[...]) * scale).astype(jnp.bfloat16)
    out_ref[:, :rows, :] = jnp.broadcast_to(sums[None], (out_ref.shape[0], rows, half))
    out_ref[:, rows:, :] = back_ref[...]


def final_kernel(all_ref, key_ref, value_ref, grad_key_ref, grad_value_ref, grad_weight_ref):
    seqs, _, half = all_ref.shape
    channels, span = key_ref.shape
    rows = channels // seqs
    for source in range(seqs):
        piece = all_ref[source].astype(jnp.float32)
        place = slice(source * rows, (source + 1) * rows)
        grad_weight_ref[place, :half] = piece[:rows]
        grad_weight_ref[place, half:] = piece[rows : 2 * rows]
        mixed = piece[2 * rows :, :span] + piece[2 * rows :, span:]
        grad_key_ref[place, :] = (mixed * value_ref[place, :].astype(jnp.float32)).astype(jnp.bfloat16)
        grad_value_ref[place, :] = (mixed * key_ref[place, :].astype(jnp.float32)).astype(jnp.bfloat16)


def fixed(values):
    return pltpu.with_memory_space_constraint(values, pltpu.HBM)


def limited(mebibytes):
    return pltpu.CompilerParams(vmem_limit_bytes=mebibytes * 1024 * 1024)


def convolve(signal, filt, natural, tables):
    _, channels, _ = signal.shape
    return pl.pallas_call(
        convolve_kernel,
        out_shape=(
            jax.ShapeDtypeStruct(signal.shape, jnp.float32),
            jax.ShapeDtypeStruct((channels // BATCH, BATCH * TALL, 2 * WIDE), jnp.float32),
        ),
        scratch_shapes=[pltpu.VMEM((TALL, channels, WIDE), jnp.float32)],
        name="convolve",
        cost_estimate=pl.CostEstimate(flops=4_000_000_000, bytes_accessed=3_000_000, transcendentals=0),
    )(signal, filt, natural, *tables)


def correlate(arrived, spec, tables):
    blocks, depth, double = arrived.shape
    channels = depth * 2 // 5
    shape = (blocks, channels, double // 2)
    return pl.pallas_call(
        correlate_kernel,
        out_shape=jax.ShapeDtypeStruct((blocks, channels, double), jnp.bfloat16),
        scratch_shapes=[pltpu.VMEM(shape, jnp.float32)] * 2,
        name="correlate",
        compiler_params=limited(LIMIT),
        cost_estimate=pl.CostEstimate(flops=4_000_000_000, bytes_accessed=3_000_000, transcendentals=0),
    )(arrived, spec, *tables)


def gather_features(block, chans):
    def send(values, hop):
        return lax.ppermute(values, "chan", [(k, hop(k)) for k in range(chans)])

    def ahead(k):
        return (k + 2) % chans

    def behind(k):
        return (k - 2) % chans

    half = block.shape[0] // 2
    from_behind = send(block, ahead)
    from_ahead = send(block, behind)
    far_top = send(from_behind[:half], ahead)
    far_bottom = send(from_ahead[half:], behind)
    mine = [block, from_behind, from_ahead, far_top, far_bottom]
    return mine + [send(values, lambda k: k ^ 1) for values in mine]


def swap(blocks, axes="seq"):
    return lax.all_to_all(blocks, axes, split_axis=0, concat_axis=0, tiled=True)


def shards(query_proj, key_proj, value_proj, grad_out, out_weight, long_filter):
    rows, length = long_filter.shape
    seqs, chans, dps = lax.axis_size("seq"), lax.axis_size("chan"), lax.axis_size("dp")
    channels, span = query_proj.shape[1:]
    features = out_weight.shape[1]
    pieces = span // WIDE
    arrived = (np.arange(seqs)[None, :] * pieces + np.arange(pieces)[:, None]).reshape(-1)
    twist, there, back = make_shared()
    analyse_natural, _ = make_tables(np.arange(TALL))
    analyse, restore = make_tables(arrived)
    tables = tuple(fixed(jnp.asarray(t)) for t in (analyse, restore, twist, there, back))
    place = lax.axis_index("chan").astype(jnp.int32).reshape(1)

    blocks = gather_features(grad_out[0], chans)
    mixed_in = pl.pallas_call(
        mix_kernel,
        out_shape=jax.ShapeDtypeStruct((seqs, rows, span), jnp.float32),
        name="mix",
        compiler_params=limited(LIMIT),
    )(fixed(key_proj[0]), fixed(value_proj[0]))
    mixed_full = swap(mixed_in)
    conv_full, spec = convolve(mixed_full, long_filter, jnp.asarray(analyse_natural), tables)

    conv_out = swap(conv_full).reshape(channels, span)
    whole = pl.BlockSpec(memory_space=pltpu.VMEM)
    shape = (seqs, 3 * rows, 2 * span)
    send, grad_query = pl.pallas_call(
        middle_kernel,
        in_specs=[pl.BlockSpec(memory_space=pltpu.SMEM)] + [whole] * 13,
        out_shape=(
            jax.ShapeDtypeStruct((seqs, 2 * rows + rows // 2, 2 * span), jnp.bfloat16),
            jax.ShapeDtypeStruct((channels, span), jnp.bfloat16),
        ),
        name="middle",
        compiler_params=limited(LIMIT),
        cost_estimate=pl.CostEstimate(flops=1_200_000_000, bytes_accessed=5_000_000, transcendentals=0),
    )(place, conv_out, query_proj[0], out_weight, *blocks)
    arrived = swap(send)

    mine = pl.pallas_call(
        total_kernel,
        out_shape=jax.ShapeDtypeStruct((2 * rows, 2 * span), jnp.float32),
        name="total",
        compiler_params=limited(LIMIT),
    )(arrived)
    other = lax.ppermute(mine, "dp", [(0, 1), (1, 0)])
    back_full = correlate(arrived, spec, tables)
    scale = 1.0 / math.sqrt(dps * length)
    last = pl.pallas_call(
        lambda *refs: last_kernel(scale, *refs),
        in_specs=[whole] * 3,
        out_specs=whole,
        out_shape=jax.ShapeDtypeStruct(shape, jnp.bfloat16),
        name="last",
        compiler_params=limited(LIMIT),
    )(mine, other, back_full)
    last = swap(last)
    grad_key, grad_value, grad_weight = pl.pallas_call(
        final_kernel,
        out_shape=(
            jax.ShapeDtypeStruct((channels, span), jnp.bfloat16),
            jax.ShapeDtypeStruct((channels, span), jnp.bfloat16),
            jax.ShapeDtypeStruct((channels, features), jnp.float32),
        ),
        name="final",
        compiler_params=limited(LIMIT),
    )(last, key_proj[0], value_proj[0])
    return (grad_query[None], grad_key[None], grad_value[None], grad_weight)


def solution(mesh):
    placed = (
        P("dp", "chan", "seq"),
        P("dp", "chan", "seq"),
        P("dp", "chan", "seq"),
        P("dp", "chan", "seq"),
        P("chan", None),
        P(("chan", "seq"), None),
    )
    return jax.shard_map(
        shards,
        mesh=mesh,
        in_specs=placed,
        out_specs=(
            P("dp", "chan", "seq"),
            P("dp", "chan", "seq"),
            P("dp", "chan", "seq"),
            P("chan", None),
        ),
        check_vma=False,
    )
```
